256 devices in a mesh: row: 32 (over y, z_lo, core), col: 8 (over x, z_hi).
Axes of the slice: x: 4, y: 4, z: 8 (z_hi: 2, z_lo: 4; z = z_hi * 4 + z_lo), core: 2. Of those that a mesh axis runs over, the one named last changes fastest.
Arguments:
- frames: bfloat16 [256, 3, 12288], P('col', None, 'row'), may hold values from -6 to 6
- rotations: float32 [3, 3, 256], replicated, may hold values from -1 to 1, as said below
- inverse_cov: float32 [12288, 12288], P('row', 'col'), may hold values from -1 to 11, as said below
Outputs:
- covariance: float32 [12288, 12288], P('row', 'col')
- fitted_rotations: float32 [3, 3, 256], P(None, None, 'col')
The draws below stay inside these ranges and needn't reach their ends.
Inputs may be any that keep to these rules, and one draw needn't show every extreme that they name: `rotations`: each frame's 3 x 3 matrix is a rotation. `inverse_cov`: symmetric.
All inputs are finite; a program needn't handle non-finite values.
Results may differ from the reference program's by a relative error of at most 0.00031.
Values may be sent and summed in bfloat16 or wider, within the bound.
A program may use at most 64 MiB of HBM per device.

```python
import math
import jax
import jax.numpy as jnp
from jax import lax

ATOMS = 12288
POLAR = 12
FRAMES = 256


def euler_matrix(angles):
    cos_a, cos_b, cos_c = (jnp.cos(angles[0]), jnp.cos(angles[1]), jnp.cos(angles[2]))
    sin_a, sin_b, sin_c = (jnp.sin(angles[0]), jnp.sin(angles[1]), jnp.sin(angles[2]))
    first = jnp.stack([cos_a * cos_b, cos_a * sin_b * sin_c - sin_a * cos_c, cos_a * sin_b * cos_c + sin_a * sin_c])
    second = jnp.stack([sin_a * cos_b, sin_a * sin_b * sin_c + cos_a * cos_c, sin_a * sin_b * cos_c - cos_a * sin_c])
    third = jnp.stack([-sin_b, cos_b * sin_c, cos_b * cos_c])
    return jnp.stack([first, second, third])


def start_angles(key):
    return jax.random.uniform(jax.random.fold_in(key, 5), (3, FRAMES), jnp.float32, -math.pi, math.pi)


def unit_layout(key):
    return jax.random.uniform(jax.random.fold_in(key, 13), (3, ATOMS), jnp.float32, -1.0, 1.0)


def draw_rotations(key, part):
    truth = euler_matrix(start_angles(key))
    angle = jax.random.uniform(jax.random.fold_in(key, 7), (FRAMES,), jnp.float32, 0.2, 3.2)
    cosine = jnp.cos(angle)
    sine = jnp.sin(angle)
    third = 1.0 / 3.0
    root = 1.0 / math.sqrt(3.0)
    identity = jnp.eye(3, dtype=jnp.float32)
    cross_form = root * jnp.array([[0.0, -1.0, 1.0], [1.0, 0.0, -1.0], [-1.0, 1.0, 0.0]], jnp.float32)
    outer_form = third * jnp.ones((3, 3), jnp.float32)
    turned = identity[:, :, None] * cosine - cross_form[:, :, None] * sine + outer_form[:, :, None] * (1.0 - cosine)
    result = turned[:, 0, None, :] * truth[0][None] + turned[:, 1, None, :] * truth[1][None] + turned[:, 2, None, :] * truth[2][None]
    return result.astype(jnp.float32)


def draw_frames(key, part):
    truth = euler_matrix(start_angles(key))
    noise_key = jax.random.fold_in(key, 17)
    size_key = jax.random.fold_in(key, 19)
    unit = unit_layout(key)
    scales = jnp.array([3.5, 2.5, 1.8], jnp.float32)
    structure = scales[:, None] * unit
    spreads = jnp.exp(jax.random.uniform(size_key, (ATOMS,), jnp.float32, math.log(0.1), math.log(0.5)))
    noise = jnp.clip(jax.random.normal(noise_key, (FRAMES, 3, ATOMS), jnp.float32), -2.5, 2.5)
    turned = jnp.transpose(truth, (2, 1, 0))
    placed = turned[:, :, 0, None] * structure[0] + turned[:, :, 1, None] * structure[1] + turned[:, :, 2, None] * structure[2]
    return (placed + spreads[None, None, :] * noise).astype(jnp.bfloat16)


def draw_inverse_cov(key, part):
    noise_key = jax.random.fold_in(key, 11)
    diag_key = jax.random.fold_in(key, 23)
    unit = unit_layout(key)
    scales = jnp.array([3.5, 2.5, 1.8], jnp.float32)
    diagonal = jnp.exp(jax.random.uniform(diag_key, (ATOMS,), jnp.float32, 0.0, math.log(10.0)))
    positions = scales[:, None] * unit
    kernel_width = 0.25
    distance = (positions[0][:, None] - positions[0][None, :]) ** 2
    distance = distance + (positions[1][:, None] - positions[1][None, :]) ** 2
    distance = distance + (positions[2][:, None] - positions[2][None, :]) ** 2
    amplitude = jnp.exp(unit[0] * unit[1])
    coupling = 0.15 * amplitude[:, None] * amplitude[None, :] * jnp.exp(distance * (-0.5 / (kernel_width * kernel_width)))
    noise = jax.random.normal(noise_key, (ATOMS, ATOMS), jnp.float32)
    symmetric = (noise + noise.T) * (0.5 * ATOMS ** (-0.5))
    rows_idx = lax.broadcasted_iota(jnp.int32, (ATOMS, ATOMS), 0)
    cols_idx = lax.broadcasted_iota(jnp.int32, (ATOMS, ATOMS), 1)
    same = rows_idx == cols_idx
    return symmetric + jnp.where(same, diagonal[:, None], coupling)


def setup_inputs(seed: int = 0) -> dict:
    arg_keys = jax.random.split(jax.random.key(seed), 4)
    return {
        "frames": draw_frames(jax.random.fold_in(arg_keys[3], 71), 0),
        "rotations": draw_rotations(jax.random.fold_in(arg_keys[3], 71), 0),
        "inverse_cov": draw_inverse_cov(jax.random.fold_in(arg_keys[3], 71), 0),
    }


def orthogonalize(fitted):
    scaling = jnp.sqrt(1.0 + lax.optimization_barrier(jnp.sum(fitted * fitted, axis=(0, 1))))
    current = jnp.transpose(fitted, (1, 0, 2)) / scaling
    for sweep in range(POLAR):
        square = jnp.einsum('ijf,kjf->ikf', current, current, precision=lax.Precision.HIGHEST)
        cubed_term = jnp.einsum('ikf,klf->ilf', square, current, precision=lax.Precision.HIGHEST)
        current = 1.5 * current - 0.5 * cubed_term
    return current

def reference(frames, rotations, inverse_cov):
    coords = frames.astype(jnp.float32)
    centre = jnp.einsum('klf,fla->ka', rotations, coords, precision=lax.Precision.HIGHEST) / FRAMES
    weighted = jnp.dot(centre, inverse_cov.T, precision=lax.Precision.HIGHEST)
    fitted = jnp.einsum('fka,la->klf', coords, weighted, precision=lax.Precision.HIGHEST)
    fitted_rotations = orthogonalize(fitted)
    moved = jnp.einsum('klf,fla->fka', fitted_rotations, coords, precision=lax.Precision.HIGHEST)
    deviation = (moved - centre[None]).astype(jnp.bfloat16)
    flat_dev = deviation.reshape(3 * FRAMES, ATOMS).astype(jnp.float32)
    covariance = jnp.dot(flat_dev.T, flat_dev, precision=lax.Precision.HIGHEST) / (3 * FRAMES)
    return (covariance, fitted_rotations)
```

```python
import functools

import jax
import jax.numpy as jnp
from jax import lax
from jax.experimental import pallas as pl
from jax.experimental.pallas import tpu as pltpu
from jax.sharding import PartitionSpec as P

POLAR = 12
ROWS = 32
COLS = 8
FB = 32
SUB = 4
ATOMS_LOCAL = 384
FRAMES = ROWS * COLS
MESH = pl.DeviceIdType.MESH
F32 = jnp.float32
BF16 = jnp.bfloat16


def split3(value):
    high = value.astype(BF16)
    rest = value - high.astype(F32)
    middle = rest.astype(BF16)
    low = (rest - middle.astype(F32)).astype(BF16)
    return high, middle, low


def contract(left, right, dims):
    return lax.dot_general(left, right, (dims, ((), ())), preferred_element_type=F32)


def remote(src, dst, send, recv, row, col):
    return pltpu.make_async_remote_copy(
        src_ref=src, dst_ref=dst, send_sem=send, recv_sem=recv, device_id=(row, col), device_id_type=MESH
    )


def polar_all(fit):
    total = jnp.zeros_like(fit[0][0])
    for k in range(3):
        for l in range(3):
            total = total + fit[k][l] * fit[k][l]
    scaling = jnp.sqrt(1.0 + total)
    cur = [[fit[k][i] / scaling for k in range(3)] for i in range(3)]
    for _ in range(POLAR):
        square = [[None] * 3 for _ in range(3)]
        for i in range(3):
            for k in range(i, 3):
                value = cur[i][0] * cur[k][0] + cur[i][1] * cur[k][1] + cur[i][2] * cur[k][2]
                square[i][k] = value
                square[k][i] = value
        nxt = [[None] * 3 for _ in range(3)]
        for i in range(3):
            for l in range(3):
                cubed = square[i][0] * cur[0][l] + square[i][1] * cur[1][l] + square[i][2] * cur[2][l]
                nxt[i][l] = 1.5 * cur[i][l] - 0.5 * cubed
        cur = nxt
    return cur


def kernel(
    x_ref, rot_ref, w_hbm, cov_hbm, tr_ref,
    wv, cpart, cbuf, wsend, wbuf, fsend, fbuf, gsend, gbuf, rbuf, pbuf, acc, coef, wide, dev_rows, dev_q, out,
    w_sem, out_sem, c_send, c_recv, w_send, w_recv, f_send, f_recv, g_send, g_recv, r_send, r_recv, p_send, p_recv,
    s_send, s_recv,
):
    row = lax.axis_index("row")
    col = lax.axis_index("col")
    core = row % 2
    sibling = row + 1 - 2 * core
    panel_col = row // SUB
    sub = row % SUB
    is_self = panel_col == col

    w_copy = pltpu.make_async_copy(w_hbm, wv, w_sem)
    w_copy.start()

    barrier = pltpu.get_barrier_semaphore()

    def greet(r, c):
        pl.semaphore_signal(barrier, inc=1, device_id=(r, c), device_id_type=MESH)

    def greet_panel(m, carry):
        r = SUB * col + m // COLS
        c = m % COLS

        @pl.when(jnp.logical_or(r != row, c != col))
        def _():
            greet(r, c)

        return carry

    lax.fori_loop(0, 32, greet_panel, 0)
    lax.fori_loop(1, COLS, lambda m, t: (greet(row, (col + m) % COLS), t)[1], 0)
    lax.fori_loop(1, ROWS, lambda m, t: (greet((row + m) % ROWS, col), t)[1], 0)

    part = jnp.zeros((3, ATOMS_LOCAL), F32)
    for l in range(3):
        whole = rot_ref[:, l, :]
        mine = jnp.zeros((3, FB), F32)
        for i in range(COLS):
            mine = mine + jnp.where(col == i, whole[:, i * FB : (i + 1) * FB], 0.0)
        block = x_ref[l * FB : (l + 1) * FB, :]
        for piece in split3(mine):
            part = part + contract(piece, block, ((1,), (0,)))
    cpart[...] = part
    rbuf[col] = x_ref[...]

    @pl.when(is_self)
    def _():
        cbuf[sub, col] = part
        pbuf[sub, col] = x_ref[...]

    pl.semaphore_wait(barrier, 70 - is_self.astype(jnp.int32))

    def centre_copy(m):
        r = (row + m) % ROWS
        return r, remote(cpart, cbuf.at[sub, col], c_send.at[m], c_recv.at[sub, col], r, panel_col)

    def centre_start(m, carry):
        r, copy = centre_copy(m)

        @pl.when(jnp.logical_or(r != row, jnp.logical_not(is_self)))
        def _():
            copy.start()

        return carry

    lax.fori_loop(0, ROWS, centre_start, 0)

    def row_copy(m):
        c = (col + m) % COLS
        return remote(x_ref, rbuf.at[col], r_send.at[m], r_recv.at[col], row, c)

    def panel_copy(m):
        r = 2 * ((row // 2 + m) % 16) + core
        return r, remote(x_ref, pbuf.at[sub, col], p_send.at[m], p_recv.at[sub, col], r, panel_col)

    def row_start(m, carry):
        row_copy(m).start()
        return carry

    def panel_start(m, carry):
        r, copy = panel_copy(m)

        @pl.when(jnp.logical_or(r != row, jnp.logical_not(is_self)))
        def _():
            copy.start()

        return carry

    lax.fori_loop(1, COLS, row_start, 0)
    lax.fori_loop(0, 16, panel_start, 0)

    def centre_wait(m, carry):
        q = m // COLS
        c = m % COLS

        @pl.when(jnp.logical_or(SUB * col + q != row, c != col))
        def _():
            remote(cpart, cbuf.at[q, c], c_send.at[0], c_recv.at[q, c], row, col).wait_recv()

        return carry

    lax.fori_loop(0, SUB * COLS, centre_wait, 0)
    centre_cols = jnp.sum(cbuf[...], axis=1) * (1.0 / FRAMES)

    w_copy.wait()
    lanes = [[centre_cols[q][l : l + 1, :] for q in range(SUB)] for l in range(3)]

    def weigh(i, carry):
        start = pl.multiple_of(i * 32, 32)
        sums = [jnp.zeros((32, 128), F32) for _ in range(3)]
        for q in range(SUB):
            for t in range(3):
                tile = wv[pl.ds(start, 32), q * 384 + t * 128 : q * 384 + (t + 1) * 128]
                for l in range(3):
                    sums[l] = sums[l] + tile * lanes[l][q][:, t * 128 : (t + 1) * 128]
        for l in range(3):
            acc[l, pl.ds(start, 32), :] = sums[l]
        return carry

    lax.fori_loop(0, 12, weigh, 0)
    ones = jnp.ones((8, 128), BF16)
    for l in range(3):
        line = jnp.zeros((8, ATOMS_LOCAL), F32)
        for piece in split3(acc[l]):
            line = line + contract(ones, piece, ((1,), (1,)))
        wsend[l : l + 1, :] = line[0:1, :]
    wsend[3:6, :] = cpart[...]
    wbuf[col] = wsend[...]

    def weight_copy(m):
        c = (col + m) % COLS
        return remote(wsend, wbuf.at[col], w_send.at[m], w_recv.at[col], row, c)

    def weight_start(m, carry):
        weight_copy(m).start()
        return carry

    def weight_wait(m, carry):
        c = (col + m) % COLS
        remote(wsend, wbuf.at[c], w_send.at[0], w_recv.at[c], row, col).wait_recv()
        return carry

    lax.fori_loop(1, COLS, weight_start, 0)
    lax.fori_loop(1, COLS, weight_wait, 0)
    both = jnp.sum(wbuf[...], axis=0)
    centre_rows = both[3:6, :] * (1.0 / FRAMES)

    fit = jnp.zeros((3, 96), F32)
    for piece in split3(both[0:3, :]):
        fit = fit + contract(piece, x_ref[...], ((1,), (1,)))
    fsend[...] = fit
    fbuf[row] = fit

    def fit_copy(m):
        r = (row + m) % ROWS
        return remote(fsend, fbuf.at[row], f_send.at[m], f_recv.at[row], r, col)

    def fit_start(m, carry):
        fit_copy(m).start()
        return carry

    def fit_wait(m, carry):
        r = (row + m) % ROWS
        remote(fsend, fbuf.at[r], f_send.at[0], f_recv.at[r], row, col).wait_recv()
        return carry

    lax.fori_loop(1, ROWS, fit_start, 0)
    lax.fori_loop(1, ROWS, fit_wait, 0)
    fitted = jnp.sum(fbuf[...], axis=0)
    gsend[...] = fitted
    gbuf[col] = fitted

    def gather_copy(m):
        c = (col + m) % COLS
        return remote(gsend, gbuf.at[col], g_send.at[m], g_recv.at[col], row, c)

    def gather_start(m, carry):
        gather_copy(m).start()
        return carry

    def gather_wait(m, carry):
        c = (col + m) % COLS
        remote(gsend, gbuf.at[c], g_send.at[0], g_recv.at[c], row, col).wait_recv()
        return carry

    lax.fori_loop(1, COLS, gather_start, 0)

    def panel_wait(m, carry):
        q = core + 2 * (m // COLS)
        c = m % COLS

        @pl.when(jnp.logical_or(SUB * col + q != row, c != col))
        def _():
            remote(x_ref, pbuf.at[q, c], p_send.at[0], p_recv.at[q, c], row, col).wait_recv()

        return carry

    def share_copy(j):
        q = core + 2 * j
        return remote(pbuf.at[q], pbuf.at[q], s_send.at[j], s_recv.at[q], sibling, col)

    for j in range(2):
        lax.fori_loop(j * COLS, (j + 1) * COLS, panel_wait, 0)
        share_copy(j).start()

    lax.fori_loop(1, COLS, gather_wait, 0)

    rows_of = [gbuf[:, l, :] for l in range(3)]
    turned = polar_all([[rows_of[l][:, k * FB : (k + 1) * FB] for l in range(3)] for k in range(3)])
    at_col = lax.broadcasted_iota(jnp.int32, (COLS, FB), 0) == col
    for k in range(3):
        for l in range(3):
            tr_ref[k, l : l + 1, :] = jnp.sum(jnp.where(at_col, turned[k][l], 0.0), axis=0, keepdims=True)
            coef[:, 0:FB] = turned[k][l]
            upright = jnp.transpose(coef[...])
            for c in range(COLS):
                wide[3 * k + l, c] = jnp.broadcast_to(upright[0:FB, c : c + 1], (FB, 128))

    def row_wait(m, carry):
        c = (col + m) % COLS
        remote(x_ref, rbuf.at[c], r_send.at[0], r_recv.at[c], row, col).wait_recv()
        return carry

    lax.fori_loop(1, COLS, row_wait, 0)

    def deviate(source, centre):
        base = [jnp.broadcast_to(centre[k : k + 1, :], (FB, ATOMS_LOCAL)) for k in range(3)]

        def body(c, carry):
            block = source[c].astype(F32)
            xs = [block[l * FB : (l + 1) * FB, :] for l in range(3)]
            start = pl.multiple_of(c * 96, 96)
            values = []
            for k in range(3):
                terms = []
                for l in range(3):
                    factor = wide[3 * k + l, c]
                    terms.append(jnp.concatenate([factor, factor, factor], axis=1) * xs[l])
                values.append((terms[0] + terms[1]) + terms[2] - base[k])
            dev_q[pl.ds(start, 96), :] = jnp.concatenate(values, axis=0).astype(BF16)
            return carry

        lax.fori_loop(0, COLS, body, 0)

    deviate(rbuf, centre_rows)
    dev_rows[...] = jnp.transpose(dev_q[...])

    for j in range(2):
        q = 1 - core + 2 * j
        remote(pbuf.at[q], pbuf.at[q], s_send.at[0], s_recv.at[q], row, col).wait_recv()

    def out_copy(q):
        return pltpu.make_async_copy(
            out.at[q], cov_hbm.at[:, pl.ds(pl.multiple_of(q * ATOMS_LOCAL, ATOMS_LOCAL), ATOMS_LOCAL)], out_sem.at[q]
        )

    for q in range(SUB):
        deviate(pbuf.at[q], centre_cols[q])
        out[q] = contract(dev_rows[...], dev_q[...], ((1,), (0,))) * (1.0 / (3 * FRAMES))
        out_copy(q).start()

    for q in range(SUB):
        out_copy(q).wait()

    def centre_sent(m, carry):
        r, copy = centre_copy(m)

        @pl.when(jnp.logical_or(r != row, jnp.logical_not(is_self)))
        def _():
            copy.wait_send()

        return carry

    def panel_sent(m, carry):
        r, copy = panel_copy(m)

        @pl.when(jnp.logical_or(r != row, jnp.logical_not(is_self)))
        def _():
            copy.wait_send()

        return carry

    lax.fori_loop(0, ROWS, centre_sent, 0)
    lax.fori_loop(0, 16, panel_sent, 0)
    for copy_of, count in ((row_copy, COLS), (weight_copy, COLS), (fit_copy, ROWS), (gather_copy, COLS)):
        lax.fori_loop(1, count, lambda m, t, f=copy_of: (f(m).wait_send(), t)[1], 0)
    for j in range(2):
        share_copy(j).wait_send()


def per_device(frames, rotations, inverse_cov):
    x = jnp.transpose(frames, (1, 0, 2)).reshape(96, ATOMS_LOCAL)
    dma = pltpu.SemaphoreType.DMA
    vmem = pl.BlockSpec(memory_space=pltpu.VMEM)
    hbm = pl.BlockSpec(memory_space=pl.ANY)
    return pl.pallas_call(
        kernel,
        out_shape=(
            jax.ShapeDtypeStruct((ATOMS_LOCAL, SUB * ATOMS_LOCAL), F32),
            jax.ShapeDtypeStruct((3, 3, FB), F32),
        ),
        in_specs=[vmem, vmem, hbm],
        out_specs=(hbm, vmem),
        scratch_shapes=[
            pltpu.VMEM((384, 1536), F32),
            pltpu.VMEM((3, 384), F32),
            pltpu.VMEM((4, 8, 3, 384), F32),
            pltpu.VMEM((6, 384), F32),
            pltpu.VMEM((8, 6, 384), F32),
            pltpu.VMEM((3, 96), F32),
            pltpu.VMEM((32, 3, 96), F32),
            pltpu.VMEM((3, 96), F32),
            pltpu.VMEM((8, 3, 96), F32),
            pltpu.VMEM((8, 96, 384), BF16),
            pltpu.VMEM((4, 8, 96, 384), BF16),
            pltpu.VMEM((3, 384, 128), F32),
            pltpu.VMEM((8, 128), F32),
            pltpu.VMEM((9, 8, 32, 128), F32),
            pltpu.VMEM((384, 768), BF16),
            pltpu.VMEM((768, 384), BF16),
            pltpu.VMEM((4, 384, 384), F32),
            dma(()), dma((4,)),
            dma((32,)), dma((4, 8)),
            dma((8,)), dma((8,)),
            dma((32,)), dma((32,)),
            dma((8,)), dma((8,)),
            dma((8,)), dma((8,)),
            dma((16,)), dma((4, 8)),
            dma((2,)), dma((4,)),
        ],
        compiler_params=pltpu.CompilerParams(
            collective_id=0, has_side_effects=True, vmem_limit_bytes=48 * 1024 * 1024
        ),
        name="superpose",
    )(x, rotations, inverse_cov)


def solution(mesh):
    placed = (P("col", None, "row"), P(), P("row", "col"))
    return jax.shard_map(
        per_device,
        mesh=mesh,
        in_specs=placed,
        out_specs=(P("row", "col"), P(None, None, "col")),
        check_vma=False,
    )
```

```python
import functools

import jax
import jax.numpy as jnp
from jax import lax
from jax.experimental import pallas as pl
from jax.experimental.pallas import tpu as pltpu
from jax.sharding import PartitionSpec as P

POLAR = 12
ROWS = 32
COLS = 8
FB = 32
SUB = 4
ATOMS_LOCAL = 384
FRAMES = ROWS * COLS
MESH = pl.DeviceIdType.MESH
F32 = jnp.float32
BF16 = jnp.bfloat16


def split3(value):
    high = value.astype(BF16)
    rest = value - high.astype(F32)
    middle = rest.astype(BF16)
    low = (rest - middle.astype(F32)).astype(BF16)
    return high, middle, low


def contract(left, right, dims):
    return lax.dot_general(left, right, (dims, ((), ())), preferred_element_type=F32)


def remote(src, dst, send, recv, row, col):
    return pltpu.make_async_remote_copy(
        src_ref=src, dst_ref=dst, send_sem=send, recv_sem=recv, device_id=(row, col), device_id_type=MESH
    )


def polar_all(fit):
    total = jnp.zeros_like(fit[0][0])
    for k in range(3):
        for l in range(3):
            total = total + fit[k][l] * fit[k][l]
    scaling = jnp.sqrt(1.0 + total)
    cur = [[fit[k][i] / scaling for k in range(3)] for i in range(3)]
    for _ in range(POLAR):
        square = [[None] * 3 for _ in range(3)]
        for i in range(3):
            for k in range(i, 3):
                value = cur[i][0] * cur[k][0] + cur[i][1] * cur[k][1] + cur[i][2] * cur[k][2]
                square[i][k] = value
                square[k][i] = value
        nxt = [[None] * 3 for _ in range(3)]
        for i in range(3):
            for l in range(3):
                cubed = square[i][0] * cur[0][l] + square[i][1] * cur[1][l] + square[i][2] * cur[2][l]
                nxt[i][l] = 1.5 * cur[i][l] - 0.5 * cubed
        cur = nxt
    return cur


def kernel(
    x_ref, rot_ref, w_hbm, cov_hbm, tr_ref,
    wv, cpart, cbuf, wsend, wbuf, fsend, fbuf, gsend, gbuf, rbuf, ybuf, pbuf, acc, coef, wide, dev_rows, dev_q, out,
    w_sem, out_sem, c_send, c_recv, w_send, w_recv, f_send, f_recv, g_send, g_recv, r_send, r_recv, z_send, z_recv,
    y_send, y_recv, x_send, x_recv, s_send, s_recv,
):
    row = lax.axis_index("row")
    col = lax.axis_index("col")
    core = row % 2
    sibling = row + 1 - 2 * core
    panel_col = row // SUB
    sub = row % SUB
    is_self = panel_col == col
    y, zl = row // 8, lax.rem(row // 2, 4)
    x, zh = col // 2, lax.rem(col, 2)
    half = zl // 2
    in_half = half == zh

    def dev(x, y, zh, zl):
        return (lax.rem(y, 4) * 4 + lax.rem(zl, 4)) * 2 + core, lax.rem(x, 4) * 2 + zh

    w_copy = pltpu.make_async_copy(w_hbm, wv, w_sem)
    w_copy.start()

    barrier = pltpu.get_barrier_semaphore()

    def greet(r, c):
        pl.semaphore_signal(barrier, inc=1, device_id=(r, c), device_id_type=MESH)

    def greet_panel(m, carry):
        r = SUB * col + m // COLS
        c = m % COLS

        @pl.when(jnp.logical_or(r != row, c != col))
        def _():
            greet(r, c)

        return carry

    lax.fori_loop(0, 32, greet_panel, 0)
    lax.fori_loop(1, COLS, lambda m, t: (greet(row, (col + m) % COLS), t)[1], 0)
    lax.fori_loop(1, ROWS, lambda m, t: (greet((row + m) % ROWS, col), t)[1], 0)
    for i in range(1, 4):
        greet(*dev(x, y, 1 - zh, zl + i))

    part = jnp.zeros((3, ATOMS_LOCAL), F32)
    for l in range(3):
        whole = rot_ref[:, l, :]
        mine = jnp.zeros((3, FB), F32)
        for i in range(COLS):
            mine = mine + jnp.where(col == i, whole[:, i * FB : (i + 1) * FB], 0.0)
        block = x_ref[l * FB : (l + 1) * FB, :]
        for piece in split3(mine):
            part = part + contract(piece, block, ((1,), (0,)))
    cpart[...] = part
    rbuf[col] = x_ref[...]

    @pl.when(is_self)
    def _():
        cbuf[sub, col] = part

    @pl.when(in_half)
    def _():
        ybuf[y, 2 * (zl % 2) + zh] = x_ref[...]

    pl.semaphore_wait(barrier, 73 - is_self.astype(jnp.int32))

    def z_copy(i):
        return remote(x_ref, ybuf.at[y, 2 * (zl % 2) + zh], z_send.at[i], z_recv.at[zl % 2, zh], *dev(x, y, half, zl + i))

    def pair_copy():
        return remote(x_ref, rbuf.at[col], z_send.at[0], r_recv.at[col], *dev(x, y, 1 - zh, zl))

    def row_copy(i, other):
        slot = 2 * x + (1 - zh if other else zh)
        source = rbuf.at[slot] if other else x_ref
        return remote(source, rbuf.at[slot], r_send.at[int(other), i], r_recv.at[slot], *dev(x + i, y, zh, zl))

    def y_copy(i, k):
        return remote(ybuf.at[y, k], ybuf.at[y, k], y_send.at[i, k], y_recv.at[y, k], *dev(x, y + i, zh, zl))

    def x_copy(i, k):
        there = lax.rem(x + i, 4)
        return remote(ybuf.at[there, k], pbuf.at[core, k, x], x_send.at[i, k], x_recv.at[k, x], *dev(there, y, zh, zl))

    def share_copy(k):
        return remote(pbuf.at[core, k], pbuf.at[core, k], s_send.at[k], s_recv.at[k], sibling, col)

    def chunk(n):
        return 2 * (n % 2) + (zh if n < 2 else 1 - zh)

    def y_step(n):
        k = chunk(n)

        @pl.when(jnp.logical_or(jnp.logical_not(in_half), zl % 2 != n % 2))
        def _():
            remote(x_ref, ybuf.at[y, k], z_send.at[0], z_recv.at[k // 2, k % 2], row, col).wait_recv()

        for i in range(1, 4):
            y_copy(i, k).start()

    def x_step(n):
        k = chunk(n)
        for i in range(1, 4):
            there = lax.rem(x + i, 4)

            @pl.when(there != y)
            def _():
                remote(x_ref, ybuf.at[there, k], y_send.at[0, 0], y_recv.at[there, k], row, col).wait_recv()

            x_copy(i, k).start()

        @pl.when(x != y)
        def _():
            remote(x_ref, ybuf.at[x, k], y_send.at[0, 0], y_recv.at[x, k], row, col).wait_recv()

        pbuf[core, k, x] = ybuf[x, k]

    def share_step(n):
        k = chunk(n)
        for i in range(1, 4):
            there = lax.rem(x + i, 4)
            remote(x_ref, pbuf.at[core, k, there], x_send.at[0, 0], x_recv.at[k, there], row, col).wait_recv()
        share_copy(k).start()

    pair_copy().start()
    for i in range(1, 4):
        z_copy(i).start()
    for i in range(1, 4):
        row_copy(i, False).start()

    def centre_copy(m):
        r = (row + m) % ROWS
        return r, remote(cpart, cbuf.at[sub, col], c_send.at[m], c_recv.at[sub, col], r, panel_col)

    def centre_start(m, carry):
        r, copy = centre_copy(m)

        @pl.when(jnp.logical_or(r != row, jnp.logical_not(is_self)))
        def _():
            copy.start()

        return carry

    lax.fori_loop(0, ROWS, centre_start, 0)

    other_slot = 2 * x + 1 - zh
    remote(x_ref, rbuf.at[other_slot], z_send.at[0], r_recv.at[other_slot], row, col).wait_recv()
    for i in range(1, 4):
        row_copy(i, True).start()

    @pl.when(in_half)
    def _():
        ybuf[y, 2 * (zl % 2) + 1 - zh] = rbuf[other_slot]

    for n in range(4):
        y_step(n)

    def centre_wait(m, carry):
        q = m // COLS
        c = m % COLS

        @pl.when(jnp.logical_or(SUB * col + q != row, c != col))
        def _():
            remote(cpart, cbuf.at[q, c], c_send.at[0], c_recv.at[q, c], row, col).wait_recv()

        return carry

    lax.fori_loop(0, SUB * COLS, centre_wait, 0)
    centre_cols = jnp.sum(cbuf[...], axis=1) * (1.0 / FRAMES)

    w_copy.wait()
    lanes = [[centre_cols[q][l : l + 1, :] for q in range(SUB)] for l in range(3)]

    def weigh(i, carry):
        start = pl.multiple_of(i * 32, 32)
        sums = [jnp.zeros((32, 128), F32) for _ in range(3)]
        for q in range(SUB):
            for t in range(3):
                tile = wv[pl.ds(start, 32), q * 384 + t * 128 : q * 384 + (t + 1) * 128]
                for l in range(3):
                    sums[l] = sums[l] + tile * lanes[l][q][:, t * 128 : (t + 1) * 128]
        for l in range(3):
            acc[l, pl.ds(start, 32), :] = sums[l]
        return carry

    lax.fori_loop(0, 12, weigh, 0)
    ones = jnp.ones((8, 128), BF16)
    for l in range(3):
        line = jnp.zeros((8, ATOMS_LOCAL), F32)
        for piece in split3(acc[l]):
            line = line + contract(ones, piece, ((1,), (1,)))
        wsend[l : l + 1, :] = line[0:1, :]
    wsend[3:6, :] = cpart[...]
    wbuf[col] = wsend[...]

    def weight_copy(m):
        c = (col + m) % COLS
        return remote(wsend, wbuf.at[col], w_send.at[m], w_recv.at[col], row, c)

    def weight_start(m, carry):
        weight_copy(m).start()
        return carry

    def weight_wait(m, carry):
        c = (col + m) % COLS
        remote(wsend, wbuf.at[c], w_send.at[0], w_recv.at[c], row, col).wait_recv()
        return carry

    lax.fori_loop(1, COLS, weight_start, 0)
    x_step(0)
    x_step(1)
    lax.fori_loop(1, COLS, weight_wait, 0)
    both = jnp.sum(wbuf[...], axis=0)
    centre_rows = both[3:6, :] * (1.0 / FRAMES)

    fit = jnp.zeros((3, 96), F32)
    for piece in split3(both[0:3, :]):
        fit = fit + contract(piece, x_ref[...], ((1,), (1,)))
    fsend[...] = fit
    fbuf[row] = fit

    def fit_copy(m):
        r = (row + m) % ROWS
        return remote(fsend, fbuf.at[row], f_send.at[m], f_recv.at[row], r, col)

    def fit_start(m, carry):
        fit_copy(m).start()
        return carry

    def fit_wait(m, carry):
        r = (row + m) % ROWS
        remote(fsend, fbuf.at[r], f_send.at[0], f_recv.at[r], row, col).wait_recv()
        return carry

    lax.fori_loop(1, ROWS, fit_start, 0)
    x_step(2)
    x_step(3)
    lax.fori_loop(1, ROWS, fit_wait, 0)
    fitted = jnp.sum(fbuf[...], axis=0)
    gsend[...] = fitted
    gbuf[col] = fitted

    def gather_copy(m):
        c = (col + m) % COLS
        return remote(gsend, gbuf.at[col], g_send.at[m], g_recv.at[col], row, c)

    def gather_start(m, carry):
        gather_copy(m).start()
        return carry

    def gather_wait(m, carry):
        c = (col + m) % COLS
        remote(gsend, gbuf.at[c], g_send.at[0], g_recv.at[c], row, col).wait_recv()
        return carry

    lax.fori_loop(1, COLS, gather_start, 0)

    for n in range(4):
        share_step(n)

    lax.fori_loop(1, COLS, gather_wait, 0)

    rows_of = [gbuf[:, l, :] for l in range(3)]
    turned = polar_all([[rows_of[l][:, k * FB : (k + 1) * FB] for l in range(3)] for k in range(3)])
    at_col = lax.broadcasted_iota(jnp.int32, (COLS, FB), 0) == col
    for k in range(3):
        for l in range(3):
            tr_ref[k, l : l + 1, :] = jnp.sum(jnp.where(at_col, turned[k][l], 0.0), axis=0, keepdims=True)
            coef[:, 0:FB] = turned[k][l]
            upright = jnp.transpose(coef[...])
            for c in range(COLS):
                wide[3 * k + l, c] = jnp.broadcast_to(upright[0:FB, c : c + 1], (FB, 128))

    for i in range(1, 4):
        for h in range(2):
            slot = 2 * lax.rem(x + i, 4) + h
            remote(x_ref, rbuf.at[slot], r_send.at[0, 0], r_recv.at[slot], row, col).wait_recv()

    def deviate(block_of, centre):
        base = [jnp.broadcast_to(centre[k : k + 1, :], (FB, ATOMS_LOCAL)) for k in range(3)]

        def body(c, carry):
            block = block_of(c).astype(F32)
            xs = [block[l * FB : (l + 1) * FB, :] for l in range(3)]
            start = pl.multiple_of(c * 96, 96)
            values = []
            for k in range(3):
                terms = []
                for l in range(3):
                    factor = wide[3 * k + l, c]
                    terms.append(jnp.concatenate([factor, factor, factor], axis=1) * xs[l])
                values.append((terms[0] + terms[1]) + terms[2] - base[k])
            dev_q[pl.ds(start, 96), :] = jnp.concatenate(values, axis=0).astype(BF16)
            return carry

        lax.fori_loop(0, COLS, body, 0)

    deviate(lambda c: rbuf[c], centre_rows)
    dev_rows[...] = jnp.transpose(dev_q[...])

    def out_copy(q):
        start = pl.multiple_of(q * ATOMS_LOCAL, ATOMS_LOCAL)
        return pltpu.make_async_copy(out.at[q], cov_hbm.at[:, pl.ds(start, ATOMS_LOCAL)], out_sem.at[q])

    for side in range(2):
        owner = core if side == 0 else 1 - core
        if side:
            for n in range(4):
                k = chunk(n)
                remote(pbuf.at[owner, k], pbuf.at[owner, k], s_send.at[0], s_recv.at[k], row, col).wait_recv()
        for j in range(2):
            q = 2 * j + owner
            centre_q = jnp.where(owner == 0, centre_cols[2 * j], centre_cols[2 * j + 1])
            deviate(lambda c: pbuf[owner, 2 * j + lax.rem(c, 2), c // 2], centre_q)
            out[q] = contract(dev_rows[...], dev_q[...], ((1,), (0,))) * (1.0 / (3 * FRAMES))
            out_copy(q).start()

    for q in range(SUB):
        out_copy(q).wait()

    def centre_sent(m, carry):
        r, copy = centre_copy(m)

        @pl.when(jnp.logical_or(r != row, jnp.logical_not(is_self)))
        def _():
            copy.wait_send()

        return carry

    lax.fori_loop(0, ROWS, centre_sent, 0)
    for copy_of, count in ((weight_copy, COLS), (fit_copy, ROWS), (gather_copy, COLS)):
        lax.fori_loop(1, count, lambda m, t, f=copy_of: (f(m).wait_send(), t)[1], 0)
    pair_copy().wait_send()
    for i in range(1, 4):
        z_copy(i).wait_send()
        row_copy(i, False).wait_send()
        row_copy(i, True).wait_send()
        for k in range(4):
            y_copy(i, k).wait_send()
            x_copy(i, k).wait_send()
    for k in range(4):
        share_copy(k).wait_send()


def per_device(frames, rotations, inverse_cov):
    x = jnp.transpose(frames, (1, 0, 2)).reshape(96, ATOMS_LOCAL)
    dma = pltpu.SemaphoreType.DMA
    vmem = pl.BlockSpec(memory_space=pltpu.VMEM)
    hbm = pl.BlockSpec(memory_space=pl.ANY)
    return pl.pallas_call(
        kernel,
        out_shape=(
            jax.ShapeDtypeStruct((ATOMS_LOCAL, SUB * ATOMS_LOCAL), F32),
            jax.ShapeDtypeStruct((3, 3, FB), F32),
        ),
        in_specs=[vmem, vmem, hbm],
        out_specs=(hbm, vmem),
        scratch_shapes=[
            pltpu.VMEM((384, 1536), F32),
            pltpu.VMEM((3, 384), F32),
            pltpu.VMEM((4, 8, 3, 384), F32),
            pltpu.VMEM((6, 384), F32),
            pltpu.VMEM((8, 6, 384), F32),
            pltpu.VMEM((3, 96), F32),
            pltpu.VMEM((32, 3, 96), F32),
            pltpu.VMEM((3, 96), F32),
            pltpu.VMEM((8, 3, 96), F32),
            pltpu.VMEM((8, 96, 384), BF16),
            pltpu.VMEM((4, 4, 96, 384), BF16),
            pltpu.VMEM((2, 4, 4, 96, 384), BF16),
            pltpu.VMEM((3, 384, 128), F32),
            pltpu.VMEM((8, 128), F32),
            pltpu.VMEM((9, 8, 32, 128), F32),
            pltpu.VMEM((384, 768), BF16),
            pltpu.VMEM((768, 384), BF16),
            pltpu.VMEM((4, 384, 384), F32),
            dma(()), dma((4,)),
            dma((32,)), dma((4, 8)),
            dma((8,)), dma((8,)),
            dma((32,)), dma((32,)),
            dma((8,)), dma((8,)),
            dma((2, 4)), dma((8,)),
            dma((4,)), dma((2, 2)),
            dma((4, 4)), dma((4, 4)),
            dma((4, 4)), dma((4, 4)),
            dma((4,)), dma((4,)),
        ],
        compiler_params=pltpu.CompilerParams(
            collective_id=0, has_side_effects=True, vmem_limit_bytes=48 * 1024 * 1024
        ),
        name="superpose",
    )(x, rotations, inverse_cov)


def solution(mesh):
    placed = (P("col", None, "row"), P(), P("row", "col"))
    return jax.shard_map(
        per_device,
        mesh=mesh,
        in_specs=placed,
        out_specs=(P("row", "col"), P(None, None, "col")),
        check_vma=False,
    )
```

```python
import functools

import jax
import jax.numpy as jnp
from jax import lax
from jax.experimental import pallas as pl
from jax.experimental.pallas import tpu as pltpu
from jax.sharding import PartitionSpec as P

POLAR = 12
ROWS = 32
COLS = 8
FB = 32
SUB = 4
ATOMS_LOCAL = 384
FRAMES = ROWS * COLS
MESH = pl.DeviceIdType.MESH
F32 = jnp.float32
BF16 = jnp.bfloat16


def split3(value):
    high = value.astype(BF16)
    rest = value - high.astype(F32)
    middle = rest.astype(BF16)
    low = (rest - middle.astype(F32)).astype(BF16)
    return high, middle, low


def contract(left, right, dims):
    return lax.dot_general(left, right, (dims, ((), ())), preferred_element_type=F32)


def remote(src, dst, send, recv, row, col):
    return pltpu.make_async_remote_copy(
        src_ref=src, dst_ref=dst, send_sem=send, recv_sem=recv, device_id=(row, col), device_id_type=MESH
    )


def polar_all(fit):
    total = jnp.zeros_like(fit[0][0])
    for k in range(3):
        for l in range(3):
            total = total + fit[k][l] * fit[k][l]
    scaling = jnp.sqrt(1.0 + total)
    cur = [[fit[k][i] / scaling for k in range(3)] for i in range(3)]
    for _ in range(POLAR):
        square = [[None] * 3 for _ in range(3)]
        for i in range(3):
            for k in range(i, 3):
                value = cur[i][0] * cur[k][0] + cur[i][1] * cur[k][1] + cur[i][2] * cur[k][2]
                square[i][k] = value
                square[k][i] = value
        nxt = [[None] * 3 for _ in range(3)]
        for i in range(3):
            for l in range(3):
                cubed = square[i][0] * cur[0][l] + square[i][1] * cur[1][l] + square[i][2] * cur[2][l]
                nxt[i][l] = 1.5 * cur[i][l] - 0.5 * cubed
        cur = nxt
    return cur


def kernel(
    x_hbm, rot_hbm, w_hbm, cov_hbm, tr_ref,
    rot, wv, cpart, cbuf, asend, abuf, bsend, bbuf, rbuf, ybuf, pbuf, acc, coef, wide, dev_rows, dev_q, out,
    in_sem, out_sem, c_send, c_recv, a_send, a_recv, b_send, b_recv, r_send, r_recv, z_send, z_recv,
    y_send, y_recv, x_send, x_recv, s_send, s_recv,
):
    row = lax.axis_index("row")
    col = lax.axis_index("col")
    core = row % 2
    sibling = row + 1 - 2 * core
    panel_col = row // SUB
    sub = row % SUB
    is_self = panel_col == col
    y, zl = row // 8, lax.rem(row // 2, 4)
    x, zh = col // 2, lax.rem(col, 2)
    half = zl // 2
    in_half = half == zh

    def dev(x, y, zh, zl):
        return (lax.rem(y, 4) * 4 + lax.rem(zl, 4)) * 2 + core, lax.rem(x, 4) * 2 + zh

    x_ref = rbuf.at[col]
    x_load = pltpu.make_async_copy(x_hbm, x_ref, in_sem.at[0])
    rot_load = pltpu.make_async_copy(rot_hbm, rot, in_sem.at[1])
    w_load = pltpu.make_async_copy(w_hbm, wv, in_sem.at[2])
    x_load.start()
    rot_load.start()
    w_load.start()

    place = 2 * (4 * zh + zl) + core

    def plane_peer(m):
        return dev(x + m // 4, y + m % 4, zh, zl)

    def ring_peer(m):
        there = lax.rem(place + m, 16)
        zc = there // 2
        return (y * 4 + lax.rem(zc, 4)) * 2 + lax.rem(there, 2), 2 * x + zc // 4

    barrier = pltpu.get_barrier_semaphore()

    def greet(r, c):
        pl.semaphore_signal(barrier, inc=1, device_id=(r, c), device_id_type=MESH)

    def greet_panel(m, carry):
        r = SUB * col + m // COLS
        c = lax.rem(m, COLS)

        @pl.when(jnp.logical_or(r != row, c != col))
        def _():
            greet(r, c)

        return carry

    lax.fori_loop(0, 32, greet_panel, 0)
    for m in range(1, 16):
        greet(*plane_peer(m))
        greet(*ring_peer(m))

    x_load.wait()
    rot_load.wait()
    part = jnp.zeros((3, ATOMS_LOCAL), F32)
    for l in range(3):
        whole = rot[:, l, :]
        mine = jnp.zeros((3, FB), F32)
        for i in range(COLS):
            mine = mine + jnp.where(col == i, whole[:, i * FB : (i + 1) * FB], 0.0)
        block = x_ref[l * FB : (l + 1) * FB, :]
        for piece in split3(mine):
            part = part + contract(piece, block, ((1,), (0,)))
    cpart[...] = part

    @pl.when(is_self)
    def _():
        cbuf[sub, col] = part

    @pl.when(in_half)
    def _():
        ybuf[y, 2 * (zl % 2) + zh] = x_ref[...]

    pl.semaphore_wait(barrier, 62 - is_self.astype(jnp.int32))

    def z_copy(i):
        return remote(x_ref, ybuf.at[y, 2 * (zl % 2) + zh], z_send.at[i], z_recv.at[zl % 2, zh], *dev(x, y, half, zl + i))

    def pair_copy():
        return remote(x_ref, rbuf.at[col], z_send.at[0], r_recv.at[col], *dev(x, y, 1 - zh, zl))

    def row_copy(i, other):
        slot = 2 * x + (1 - zh if other else zh)
        source = rbuf.at[slot] if other else x_ref
        return remote(source, rbuf.at[slot], r_send.at[int(other), i], r_recv.at[slot], *dev(x + i, y, zh, zl))

    def y_copy(i, k):
        return remote(ybuf.at[y, k], ybuf.at[y, k], y_send.at[i, k], y_recv.at[y, k], *dev(x, y + i, zh, zl))

    def x_copy(i, k):
        there = lax.rem(x + i, 4)
        return remote(ybuf.at[there, k], pbuf.at[core, k, x], x_send.at[i, k], x_recv.at[k, x], *dev(there, y, zh, zl))

    def share_copy(k):
        return remote(pbuf.at[core, k], pbuf.at[core, k], s_send.at[k], s_recv.at[k], sibling, col)

    def chunk(n):
        return 2 * (n % 2) + (zh if n < 2 else 1 - zh)

    def y_step(n):
        k = chunk(n)

        @pl.when(jnp.logical_or(jnp.logical_not(in_half), zl % 2 != n % 2))
        def _():
            remote(x_ref, ybuf.at[y, k], z_send.at[0], z_recv.at[k // 2, k % 2], row, col).wait_recv()

        for i in range(1, 4):
            y_copy(i, k).start()

    def x_step(n):
        k = chunk(n)
        for i in range(1, 4):
            there = lax.rem(x + i, 4)

            @pl.when(there != y)
            def _():
                remote(x_ref, ybuf.at[there, k], y_send.at[0, 0], y_recv.at[there, k], row, col).wait_recv()

            x_copy(i, k).start()

        @pl.when(x != y)
        def _():
            remote(x_ref, ybuf.at[x, k], y_send.at[0, 0], y_recv.at[x, k], row, col).wait_recv()

        pbuf[core, k, x] = ybuf[x, k]

    def share_step(n):
        k = chunk(n)
        for i in range(1, 4):
            there = lax.rem(x + i, 4)
            remote(x_ref, pbuf.at[core, k, there], x_send.at[0, 0], x_recv.at[k, there], row, col).wait_recv()
        share_copy(k).start()

    pair_copy().start()
    for i in range(1, 4):
        z_copy(i).start()
    for i in range(1, 4):
        row_copy(i, False).start()

    def centre_copy(m):
        r = (row + m) % ROWS
        return r, remote(cpart, cbuf.at[sub, col], c_send.at[m], c_recv.at[sub, col], r, panel_col)

    def centre_start(m, carry):
        r, copy = centre_copy(m)

        @pl.when(jnp.logical_or(r != row, jnp.logical_not(is_self)))
        def _():
            copy.start()

        return carry

    lax.fori_loop(0, ROWS, centre_start, 0)

    other_slot = 2 * x + 1 - zh
    remote(x_ref, rbuf.at[other_slot], z_send.at[0], r_recv.at[other_slot], row, col).wait_recv()
    for i in range(1, 4):
        row_copy(i, True).start()

    @pl.when(in_half)
    def _():
        ybuf[y, 2 * (zl % 2) + 1 - zh] = rbuf[other_slot]

    for n in range(4):
        y_step(n)

    def centre_wait(m, carry):
        q = m // COLS
        c = m % COLS

        @pl.when(jnp.logical_or(SUB * col + q != row, c != col))
        def _():
            remote(cpart, cbuf.at[q, c], c_send.at[0], c_recv.at[q, c], row, col).wait_recv()

        return carry

    lax.fori_loop(0, SUB * COLS, centre_wait, 0)
    centre_cols = jnp.sum(cbuf[...], axis=1) * (1.0 / FRAMES)

    w_load.wait()
    lanes = [[centre_cols[q][l : l + 1, :] for q in range(SUB)] for l in range(3)]

    def weigh(i, carry):
        start = pl.multiple_of(i * 32, 32)
        sums = [jnp.zeros((32, 128), F32) for _ in range(3)]
        for q in range(SUB):
            for t in range(3):
                tile = wv[pl.ds(start, 32), q * 384 + t * 128 : q * 384 + (t + 1) * 128]
                for l in range(3):
                    sums[l] = sums[l] + tile * lanes[l][q][:, t * 128 : (t + 1) * 128]
        for l in range(3):
            for p, piece in enumerate(split3(sums[l])):
                acc[pl.ds(start, 32), (3 * l + p) * 128 : (3 * l + p + 1) * 128] = piece
        return carry

    lax.fori_loop(0, 12, weigh, 0)
    shape = (8, 9 * 128)
    owner_of = lax.broadcasted_iota(jnp.int32, shape, 1) // 384
    chooser = jnp.where(owner_of == lax.broadcasted_iota(jnp.int32, shape, 0), 1.0, 0.0).astype(BF16)
    weighted = contract(chooser, acc[...], ((1,), (1,)))

    for i in range(1, 4):
        for h in range(2):
            slot = 2 * lax.rem(x + i, 4) + h
            remote(x_ref, rbuf.at[slot], r_send.at[0, 0], r_recv.at[slot], row, col).wait_recv()
    pieces = jnp.concatenate(split3(weighted), axis=0)
    for k in range(3):
        frames_k = rbuf[:, k * FB : (k + 1) * FB, :].reshape(FRAMES, ATOMS_LOCAL)
        product = contract(pieces, frames_k, ((1,), (1,)))
        asend[k] = (product[0:8] + product[8:16] + product[16:24])[0:3]
    a_slot = 4 * x + y
    abuf[a_slot] = asend[...]

    def plane_copy(m):
        return remote(asend, abuf.at[a_slot], a_send.at[m], a_recv.at[a_slot], *plane_peer(m))

    def ring_copy(m):
        return remote(bsend, bbuf.at[place], b_send.at[m], b_recv.at[place], *ring_peer(m))

    for m in range(1, 16):
        plane_copy(m).start()
    x_step(0)
    x_step(1)
    for m in range(1, 16):
        slot = 4 * lax.rem(x + m // 4, 4) + lax.rem(y + m % 4, 4)
        remote(asend, abuf.at[slot], a_send.at[0], a_recv.at[slot], row, col).wait_recv()
    partial_fit = jnp.sum(abuf[...], axis=0)
    bsend[...] = partial_fit
    bbuf[place] = partial_fit
    for m in range(1, 16):
        ring_copy(m).start()
    x_step(2)
    x_step(3)

    centre_rows = jnp.zeros((8, ATOMS_LOCAL), F32)
    for l in range(3):
        frames_l = rbuf[:, l * FB : (l + 1) * FB, :].reshape(FRAMES, ATOMS_LOCAL)
        spin = jnp.concatenate([rot[:, l, :], jnp.zeros((5, FRAMES), F32)], axis=0)
        product = contract(jnp.concatenate(split3(spin), axis=0), frames_l, ((1,), (0,)))
        centre_rows = centre_rows + (product[0:8] + product[8:16] + product[16:24])
    centre_rows = centre_rows * (1.0 / FRAMES)

    for n in range(4):
        share_step(n)

    for m in range(1, 16):
        slot = lax.rem(place + m, 16)
        remote(bsend, bbuf.at[slot], b_send.at[0], b_recv.at[slot], row, col).wait_recv()
    fitted = jnp.sum(bbuf[...], axis=0)

    turned = polar_all([[fitted[k][l : l + 1, :] for l in range(3)] for k in range(3)])
    for k in range(3):
        for l in range(3):
            coef[3 * k + l : 3 * k + l + 1, :] = turned[k][l]
    every = coef[...]
    mine = jnp.zeros((16, FB), F32)
    for i in range(COLS):
        mine = mine + jnp.where(col == i, every[:, i * FB : (i + 1) * FB], 0.0)
    for k in range(3):
        tr_ref[k] = mine[3 * k : 3 * k + 3, :]
    upright = jnp.transpose(every)
    for c in range(COLS):
        for j in range(9):
            wide[j, c] = jnp.broadcast_to(upright[c * FB : (c + 1) * FB, j : j + 1], (FB, 128))

    def deviate(block_of, centre):
        base = [jnp.broadcast_to(centre[k : k + 1, :], (FB, ATOMS_LOCAL)) for k in range(3)]

        def body(c, carry):
            block = block_of(c).astype(F32)
            xs = [block[l * FB : (l + 1) * FB, :] for l in range(3)]
            start = pl.multiple_of(c * 96, 96)
            values = []
            for k in range(3):
                terms = []
                for l in range(3):
                    factor = wide[3 * k + l, c]
                    terms.append(jnp.concatenate([factor, factor, factor], axis=1) * xs[l])
                values.append((terms[0] + terms[1]) + terms[2] - base[k])
            dev_q[pl.ds(start, 96), :] = jnp.concatenate(values, axis=0).astype(BF16)
            return carry

        lax.fori_loop(0, COLS, body, 0)

    deviate(lambda c: rbuf[c], centre_rows)
    dev_rows[...] = jnp.transpose(dev_q[...])

    def out_copy(q):
        start = pl.multiple_of(q * ATOMS_LOCAL, ATOMS_LOCAL)
        return pltpu.make_async_copy(out.at[q], cov_hbm.at[:, pl.ds(start, ATOMS_LOCAL)], out_sem.at[q])

    for side in range(2):
        owner = core if side == 0 else 1 - core
        if side:
            for n in range(4):
                k = chunk(n)
                remote(pbuf.at[owner, k], pbuf.at[owner, k], s_send.at[0], s_recv.at[k], row, col).wait_recv()
        for j in range(2):
            q = 2 * j + owner
            centre_q = jnp.where(owner == 0, centre_cols[2 * j], centre_cols[2 * j + 1])
            deviate(lambda c: pbuf[owner, 2 * j + lax.rem(c, 2), c // 2], centre_q)
            out[q] = contract(dev_rows[...], dev_q[...], ((1,), (0,))) * (1.0 / (3 * FRAMES))
            out_copy(q).start()

    for q in range(SUB):
        out_copy(q).wait()

    def centre_sent(m, carry):
        r, copy = centre_copy(m)

        @pl.when(jnp.logical_or(r != row, jnp.logical_not(is_self)))
        def _():
            copy.wait_send()

        return carry

    lax.fori_loop(0, ROWS, centre_sent, 0)
    for m in range(1, 16):
        plane_copy(m).wait_send()
        ring_copy(m).wait_send()
    pair_copy().wait_send()
    for i in range(1, 4):
        z_copy(i).wait_send()
        row_copy(i, False).wait_send()
        row_copy(i, True).wait_send()
        for k in range(4):
            y_copy(i, k).wait_send()
            x_copy(i, k).wait_send()
    for k in range(4):
        share_copy(k).wait_send()


def per_device(frames, rotations, inverse_cov):
    x = jnp.transpose(frames, (1, 0, 2)).reshape(96, ATOMS_LOCAL)
    dma = pltpu.SemaphoreType.DMA
    vmem = pl.BlockSpec(memory_space=pltpu.VMEM)
    hbm = pl.BlockSpec(memory_space=pltpu.HBM)
    return pl.pallas_call(
        kernel,
        out_shape=(
            jax.ShapeDtypeStruct((ATOMS_LOCAL, SUB * ATOMS_LOCAL), F32),
            jax.ShapeDtypeStruct((3, 3, FB), F32),
        ),
        in_specs=[hbm, hbm, hbm],
        out_specs=(pl.BlockSpec(memory_space=pl.ANY), vmem),
        scratch_shapes=[
            pltpu.VMEM((3, 3, 256), F32),
            pltpu.VMEM((384, 1536), F32),
            pltpu.VMEM((3, 384), F32),
            pltpu.VMEM((4, 8, 3, 384), F32),
            pltpu.VMEM((3, 3, 256), F32),
            pltpu.VMEM((16, 3, 3, 256), F32),
            pltpu.VMEM((3, 3, 256), F32),
            pltpu.VMEM((16, 3, 3, 256), F32),
            pltpu.VMEM((8, 96, 384), BF16),
            pltpu.VMEM((4, 4, 96, 384), BF16),
            pltpu.VMEM((2, 4, 4, 96, 384), BF16),
            pltpu.VMEM((384, 1152), BF16),
            pltpu.VMEM((16, 256), F32),
            pltpu.VMEM((9, 8, 32, 128), F32),
            pltpu.VMEM((384, 768), BF16),
            pltpu.VMEM((768, 384), BF16),
            pltpu.VMEM((4, 384, 384), F32),
            dma((3,)), dma((4,)),
            dma((32,)), dma((4, 8)),
            dma((16,)), dma((16,)),
            dma((16,)), dma((16,)),
            dma((2, 4)), dma((8,)),
            dma((4,)), dma((2, 2)),
            dma((4, 4)), dma((4, 4)),
            dma((4, 4)), dma((4, 4)),
            dma((4,)), dma((4,)),
        ],
        compiler_params=pltpu.CompilerParams(
            collective_id=0, has_side_effects=True, vmem_limit_bytes=48 * 1024 * 1024
        ),
        name="superpose",
    )(x, rotations, inverse_cov)


def solution(mesh):
    placed = (P("col", None, "row"), P(), P("row", "col"))
    return jax.shard_map(
        per_device,
        mesh=mesh,
        in_specs=placed,
        out_specs=(P("row", "col"), P(None, None, "col")),
        check_vma=False,
    )
```

```python
import functools

import jax
import jax.numpy as jnp
from jax import lax
from jax.experimental import pallas as pl
from jax.experimental.pallas import tpu as pltpu
from jax.sharding import PartitionSpec as P

POLAR = 12
ROWS = 32
COLS = 8
FB = 32
SUB = 4
ATOMS_LOCAL = 384
FRAMES = ROWS * COLS
MESH = pl.DeviceIdType.MESH
F32 = jnp.float32
BF16 = jnp.bfloat16


def split3(value):
    high = value.astype(BF16)
    rest = value - high.astype(F32)
    middle = rest.astype(BF16)
    low = (rest - middle.astype(F32)).astype(BF16)
    return high, middle, low


def contract(left, right, dims):
    return lax.dot_general(left, right, (dims, ((), ())), preferred_element_type=F32)


def remote(src, dst, send, recv, row, col):
    return pltpu.make_async_remote_copy(
        src_ref=src, dst_ref=dst, send_sem=send, recv_sem=recv, device_id=(row, col), device_id_type=MESH
    )


def polar_all(fit):
    total = jnp.zeros_like(fit[0][0])
    for k in range(3):
        for l in range(3):
            total = total + fit[k][l] * fit[k][l]
    scaling = jnp.sqrt(1.0 + total)
    cur = [[fit[k][i] / scaling for k in range(3)] for i in range(3)]
    for _ in range(POLAR):
        square = [[None] * 3 for _ in range(3)]
        for i in range(3):
            for k in range(i, 3):
                value = cur[i][0] * cur[k][0] + cur[i][1] * cur[k][1] + cur[i][2] * cur[k][2]
                square[i][k] = value
                square[k][i] = value
        nxt = [[None] * 3 for _ in range(3)]
        for i in range(3):
            for l in range(3):
                cubed = square[i][0] * cur[0][l] + square[i][1] * cur[1][l] + square[i][2] * cur[2][l]
                nxt[i][l] = 1.5 * cur[i][l] - 0.5 * cubed
        cur = nxt
    return cur


def kernel(
    x_hbm, rot_hbm, w_hbm, cov_hbm, tr_ref,
    rot, wv, cpart, cbuf, csum, hsend, hbuf, asend, abuf, bsend, bbuf, turn, rbuf, ybuf, pbuf, acc, coef, wide, dev_rows, dev_q, out,
    in_sem, out_sem, c_send, c_recv, h_send, h_recv, a_send, a_recv, b_send, b_recv, r_send, r_recv, z_send, z_recv,
    y_send, y_recv, x_send, x_recv, s_send, s_recv,
):
    row = lax.axis_index("row")
    col = lax.axis_index("col")
    core = row % 2
    sibling = row + 1 - 2 * core
    panel_col = row // SUB
    sub = row % SUB
    is_self = panel_col == col
    y, zl = row // 8, lax.rem(row // 2, 4)
    x, zh = col // 2, lax.rem(col, 2)
    half = zl // 2
    in_half = half == zh

    def dev(x, y, zh, zl):
        return (lax.rem(y, 4) * 4 + lax.rem(zl, 4)) * 2 + core, lax.rem(x, 4) * 2 + zh

    x_ref = rbuf.at[col]
    x_load = pltpu.make_async_copy(x_hbm, x_ref, in_sem.at[0])
    rot_load = pltpu.make_async_copy(rot_hbm, rot, in_sem.at[1])
    w_load = pltpu.make_async_copy(w_hbm, wv, in_sem.at[2])
    x_load.start()
    rot_load.start()
    w_load.start()

    z = 4 * zh + zl

    def plane_peer(m):
        return dev(x + m // 4, y + m % 4, zh, zl)

    def ring_peer(m):
        there = lax.rem(z + m, 8)
        return dev(x, y, there // 4, there)

    barrier = pltpu.get_barrier_semaphore()

    def greet(r, c):
        pl.semaphore_signal(barrier, inc=1, device_id=(r, c), device_id_type=MESH)

    for m in range(16):
        r = SUB * col + 2 * (m // COLS) + core
        c = m % COLS

        @pl.when(jnp.logical_or(r != row, c != col))
        def _():
            greet(r, c)

    for m in range(1, 16):
        greet(*plane_peer(m))
    for m in range(1, 8):
        greet(*ring_peer(m))
    greet(sibling, col)

    x_load.wait()
    rot_load.wait()
    part = jnp.zeros((3, ATOMS_LOCAL), F32)
    for l in range(3):
        whole = rot[:, l, :]
        mine = jnp.zeros((3, FB), F32)
        for i in range(COLS):
            mine = mine + jnp.where(col == i, whole[:, i * FB : (i + 1) * FB], 0.0)
        block = x_ref[l * FB : (l + 1) * FB, :]
        for piece in split3(mine):
            part = part + contract(piece, block, ((1,), (0,)))
    for l in range(3):
        cpart[0:1, l * ATOMS_LOCAL : (l + 1) * ATOMS_LOCAL] = part[l : l + 1, :]

    @pl.when(is_self)
    def _():
        cbuf[sub // 2, col] = cpart[...]

    @pl.when(in_half)
    def _():
        ybuf[y, 2 * (zl % 2) + zh] = x_ref[...]

    pl.semaphore_wait(barrier, 39 - is_self.astype(jnp.int32))

    def z_copy(i):
        return remote(x_ref, ybuf.at[y, 2 * (zl % 2) + zh], z_send.at[i], z_recv.at[zl % 2, zh], *dev(x, y, half, zl + i))

    def pair_copy():
        return remote(x_ref, rbuf.at[col], z_send.at[0], r_recv.at[col], *dev(x, y, 1 - zh, zl))

    def row_copy(i, other):
        slot = 2 * x + (1 - zh if other else zh)
        source = rbuf.at[slot] if other else x_ref
        return remote(source, rbuf.at[slot], r_send.at[int(other), i], r_recv.at[slot], *dev(x + i, y, zh, zl))

    def y_copy(i, k):
        return remote(ybuf.at[y, k], ybuf.at[y, k], y_send.at[i, k], y_recv.at[y, k], *dev(x, y + i, zh, zl))

    def x_copy(i, k):
        there = lax.rem(x + i, 4)
        return remote(ybuf.at[there, k], pbuf.at[core, k, x], x_send.at[i, k], x_recv.at[k, x], *dev(there, y, zh, zl))

    def share_copy(k):
        return remote(pbuf.at[core, k], pbuf.at[core, k], s_send.at[k], s_recv.at[k], sibling, col)

    def chunk(n):
        return 2 * (n % 2) + (zh if n < 2 else 1 - zh)

    def y_step(n):
        k = chunk(n)

        @pl.when(jnp.logical_or(jnp.logical_not(in_half), zl % 2 != n % 2))
        def _():
            remote(x_ref, ybuf.at[y, k], z_send.at[0], z_recv.at[k // 2, k % 2], row, col).wait_recv()

        for i in range(1, 4):
            y_copy(i, k).start()

    def x_step(n):
        k = chunk(n)
        for i in range(1, 4):
            there = lax.rem(x + i, 4)

            @pl.when(there != y)
            def _():
                remote(x_ref, ybuf.at[there, k], y_send.at[0, 0], y_recv.at[there, k], row, col).wait_recv()

            x_copy(i, k).start()

        @pl.when(x != y)
        def _():
            remote(x_ref, ybuf.at[x, k], y_send.at[0, 0], y_recv.at[x, k], row, col).wait_recv()

        pbuf[core, k, x] = ybuf[x, k]

    def share_step(n):
        k = chunk(n)
        for i in range(1, 4):
            there = lax.rem(x + i, 4)
            remote(x_ref, pbuf.at[core, k, there], x_send.at[0, 0], x_recv.at[k, there], row, col).wait_recv()
        share_copy(k).start()

    pair_copy().start()
    for i in range(1, 4):
        z_copy(i).start()
    for i in range(1, 4):
        row_copy(i, False).start()

    def centre_copy(m):
        r = 2 * lax.rem(row // 2 + m, 16) + core
        return remote(cpart, cbuf.at[sub // 2, col], c_send.at[m], c_recv.at[sub // 2, col], r, panel_col)

    for m in range(16):
        if m:
            centre_copy(m).start()
        else:

            @pl.when(jnp.logical_not(is_self))
            def _():
                centre_copy(0).start()

    other_slot = 2 * x + 1 - zh
    remote(x_ref, rbuf.at[other_slot], z_send.at[0], r_recv.at[other_slot], row, col).wait_recv()
    for i in range(1, 4):
        row_copy(i, True).start()

    @pl.when(in_half)
    def _():
        ybuf[y, 2 * (zl % 2) + 1 - zh] = rbuf[other_slot]

    y_step(0)
    y_step(1)

    for j in range(2):
        for c in range(COLS):

            @pl.when(jnp.logical_or(SUB * col + 2 * j + core != row, c != col))
            def _():
                remote(cpart, cbuf.at[j, c], c_send.at[0], c_recv.at[j, c], row, col).wait_recv()

    csum[core] = jnp.sum(cbuf[...], axis=1) * (1.0 / FRAMES)

    def half_copy(i, src, dst):
        return remote(src, dst, h_send.at[i], h_recv.at[i], sibling, col)

    centre_half = half_copy(0, csum.at[core], csum.at[core])
    centre_half.start()
    y_step(2)
    y_step(3)
    half_copy(0, csum.at[core], csum.at[1 - core]).wait_recv()

    w_load.wait()
    lanes = [[csum[q % 2, q // 2, :, l * ATOMS_LOCAL : (l + 1) * ATOMS_LOCAL] for q in range(SUB)] for l in range(3)]

    def weigh(i, carry):
        start = pl.multiple_of(i * 32, 32)
        sums = [jnp.zeros((32, 128), F32) for _ in range(3)]
        for q in range(SUB):
            for t in range(3):
                tile = wv[pl.ds(start, 32), q * 384 + t * 128 : q * 384 + (t + 1) * 128]
                for l in range(3):
                    sums[l] = sums[l] + tile * lanes[l][q][:, t * 128 : (t + 1) * 128]
        for l in range(3):
            for p, piece in enumerate(split3(sums[l])):
                acc[pl.ds(start, 32), (3 * l + p) * 128 : (3 * l + p + 1) * 128] = piece
        return carry

    lax.fori_loop(0, 12, weigh, 0)
    shape = (8, 9 * 128)
    owner_of = lax.broadcasted_iota(jnp.int32, shape, 1) // 384
    chooser = jnp.where(owner_of == lax.broadcasted_iota(jnp.int32, shape, 0), 1.0, 0.0).astype(BF16)
    weighted = contract(chooser, acc[...], ((1,), (1,)))

    for i in range(1, 4):
        for h in range(2):
            slot = 2 * lax.rem(x + i, 4) + h
            remote(x_ref, rbuf.at[slot], r_send.at[0, 0], r_recv.at[slot], row, col).wait_recv()
    pieces = jnp.concatenate(split3(weighted), axis=0)
    first = core == 0
    for k in range(3):
        frames_k = rbuf[:, k * FB : (k + 1) * FB, :].reshape(FRAMES, ATOMS_LOCAL)
        product = contract(pieces, frames_k, ((1,), (1,)))
        product = product[0:8] + product[8:16] + product[16:24]
        own = jnp.where(first, product[:, 0:128], product[:, 128:256])
        others = jnp.where(first, product[:, 128:256], product[:, 0:128])
        for l in range(3):
            at = (3 * k + l) * 128
            asend[0:1, at : at + 128] = own[l : l + 1, :]
            hsend[0:1, at : at + 128] = others[l : l + 1, :]
    fit_half = half_copy(1, hsend, hbuf.at[0])
    fit_half.start()
    x_step(0)
    fit_half.wait_recv()
    asend[...] = asend[...] + hbuf[0]
    a_slot = 4 * x + y
    abuf[a_slot] = asend[...]

    def plane_copy(m):
        return remote(asend, abuf.at[a_slot], a_send.at[m], a_recv.at[a_slot], *plane_peer(m))

    def ring_copy(m):
        return remote(bsend, bbuf.at[z], b_send.at[m], b_recv.at[z], *ring_peer(m))

    for m in range(1, 16):
        plane_copy(m).start()
    x_step(1)
    for m in range(1, 16):
        slot = 4 * lax.rem(x + m // 4, 4) + lax.rem(y + m % 4, 4)
        remote(asend, abuf.at[slot], a_send.at[0], a_recv.at[slot], row, col).wait_recv()
    bsend[...] = jnp.sum(abuf[...], axis=0)
    bbuf[z] = bsend[...]
    for m in range(1, 8):
        ring_copy(m).start()
    x_step(2)
    x_step(3)
    share_step(0)
    share_step(1)

    centre_rows = jnp.zeros((8, ATOMS_LOCAL), F32)
    for l in range(3):
        frames_l = rbuf[:, l * FB : (l + 1) * FB, :].reshape(FRAMES, ATOMS_LOCAL)
        spin = jnp.concatenate([rot[:, l, :], jnp.zeros((5, FRAMES), F32)], axis=0)
        product = contract(jnp.concatenate(split3(spin), axis=0), frames_l, ((1,), (0,)))
        centre_rows = centre_rows + (product[0:8] + product[8:16] + product[16:24])
    centre_rows = centre_rows * (1.0 / FRAMES)

    for m in range(1, 8):
        slot = lax.rem(z + m, 8)
        remote(bsend, bbuf.at[slot], b_send.at[0], b_recv.at[slot], row, col).wait_recv()
    fitted = jnp.sum(bbuf[...], axis=0)

    turned = polar_all([[fitted[:, (3 * k + l) * 128 : (3 * k + l + 1) * 128] for l in range(3)] for k in range(3)])
    for k in range(3):
        for l in range(3):
            turn[core, :, (3 * k + l) * 128 : (3 * k + l + 1) * 128] = turned[k][l]
    turn_half = half_copy(2, turn.at[core], turn.at[core])
    turn_half.start()
    share_step(2)
    half_copy(2, turn.at[core], turn.at[1 - core]).wait_recv()
    picked = jnp.where(col < 4, turn[0], turn[1])
    quarter = lax.rem(col, 4)
    for k in range(3):
        for l in range(3):
            line = picked[:, (3 * k + l) * 128 : (3 * k + l + 1) * 128]
            mine = jnp.zeros((1, FB), F32)
            for i in range(4):
                mine = mine + jnp.where(quarter == i, line[:, i * FB : (i + 1) * FB], 0.0)
            tr_ref[k, l : l + 1, :] = mine
    for half_of in range(2):
        for j in range(9):
            coef[j : j + 1, :] = turn[half_of, :, j * 128 : (j + 1) * 128]
        upright = jnp.transpose(coef[...])
        for c in range(4):
            for j in range(9):
                wide[j, 4 * half_of + c] = jnp.broadcast_to(upright[c * FB : (c + 1) * FB, j : j + 1], (FB, 128))

    def deviate(block_of, centre):
        base = [jnp.broadcast_to(centre[k], (FB, ATOMS_LOCAL)) for k in range(3)]

        def body(c, carry):
            block = block_of(c).astype(F32)
            xs = [block[l * FB : (l + 1) * FB, :] for l in range(3)]
            start = pl.multiple_of(c * 96, 96)
            values = []
            for k in range(3):
                terms = []
                for l in range(3):
                    factor = wide[3 * k + l, c]
                    terms.append(jnp.concatenate([factor, factor, factor], axis=1) * xs[l])
                values.append((terms[0] + terms[1]) + terms[2] - base[k])
            dev_q[pl.ds(start, 96), :] = jnp.concatenate(values, axis=0).astype(BF16)
            return carry

        lax.fori_loop(0, COLS, body, 0)

    deviate(lambda c: rbuf[c], [centre_rows[k : k + 1, :] for k in range(3)])
    dev_rows[...] = jnp.transpose(dev_q[...])
    share_step(3)

    def out_copy(q):
        start = pl.multiple_of(q * ATOMS_LOCAL, ATOMS_LOCAL)
        return pltpu.make_async_copy(out.at[q], cov_hbm.at[:, pl.ds(start, ATOMS_LOCAL)], out_sem.at[q])

    for side in range(2):
        owner = core if side == 0 else 1 - core
        for j in range(2):
            if side:
                for h in range(2):
                    k = 2 * j + h
                    remote(pbuf.at[owner, k], pbuf.at[owner, k], s_send.at[0], s_recv.at[k], row, col).wait_recv()
            q = 2 * j + owner
            centre_q = [csum[owner, j, :, k * ATOMS_LOCAL : (k + 1) * ATOMS_LOCAL] for k in range(3)]
            deviate(lambda c: pbuf[owner, 2 * j + lax.rem(c, 2), c // 2], centre_q)
            out[q] = contract(dev_rows[...], dev_q[...], ((1,), (0,))) * (1.0 / (3 * FRAMES))
            out_copy(q).start()

    for q in range(SUB):
        out_copy(q).wait()

    for m in range(16):
        if m:
            centre_copy(m).wait_send()
        else:

            @pl.when(jnp.logical_not(is_self))
            def _():
                centre_copy(0).wait_send()

    for m in range(1, 16):
        plane_copy(m).wait_send()
    for m in range(1, 8):
        ring_copy(m).wait_send()
    centre_half.wait_send()
    fit_half.wait_send()
    turn_half.wait_send()
    pair_copy().wait_send()
    for i in range(1, 4):
        z_copy(i).wait_send()
        row_copy(i, False).wait_send()
        row_copy(i, True).wait_send()
        for k in range(4):
            y_copy(i, k).wait_send()
            x_copy(i, k).wait_send()
    for k in range(4):
        share_copy(k).wait_send()


def per_device(frames, rotations, inverse_cov):
    x = jnp.transpose(frames, (1, 0, 2)).reshape(96, ATOMS_LOCAL)
    dma = pltpu.SemaphoreType.DMA
    vmem = pl.BlockSpec(memory_space=pltpu.VMEM)
    hbm = pl.BlockSpec(memory_space=pltpu.HBM)
    return pl.pallas_call(
        kernel,
        out_shape=(
            jax.ShapeDtypeStruct((ATOMS_LOCAL, SUB * ATOMS_LOCAL), F32),
            jax.ShapeDtypeStruct((3, 3, FB), F32),
        ),
        in_specs=[hbm, hbm, hbm],
        out_specs=(pl.BlockSpec(memory_space=pl.ANY), vmem),
        scratch_shapes=[
            pltpu.VMEM((3, 3, 256), F32),
            pltpu.VMEM((384, 1536), F32),
            pltpu.VMEM((1, 1152), F32),
            pltpu.VMEM((2, 8, 1, 1152), F32),
            pltpu.VMEM((2, 2, 1, 1152), F32),
            pltpu.VMEM((1, 1152), F32),
            pltpu.VMEM((1, 1, 1152), F32),
            pltpu.VMEM((1, 1152), F32),
            pltpu.VMEM((16, 1, 1152), F32),
            pltpu.VMEM((1, 1152), F32),
            pltpu.VMEM((8, 1, 1152), F32),
            pltpu.VMEM((2, 1, 1152), F32),
            pltpu.VMEM((8, 96, 384), BF16),
            pltpu.VMEM((4, 4, 96, 384), BF16),
            pltpu.VMEM((2, 4, 4, 96, 384), BF16),
            pltpu.VMEM((384, 1152), BF16),
            pltpu.VMEM((16, 128), F32),
            pltpu.VMEM((9, 8, 32, 128), F32),
            pltpu.VMEM((384, 768), BF16),
            pltpu.VMEM((768, 384), BF16),
            pltpu.VMEM((4, 384, 384), F32),
            dma((3,)), dma((4,)),
            dma((16,)), dma((2, 8)),
            dma((3,)), dma((3,)),
            dma((16,)), dma((16,)),
            dma((8,)), dma((8,)),
            dma((2, 4)), dma((8,)),
            dma((4,)), dma((2, 2)),
            dma((4, 4)), dma((4, 4)),
            dma((4, 4)), dma((4, 4)),
            dma((4,)), dma((4,)),
        ],
        compiler_params=pltpu.CompilerParams(
            collective_id=0, has_side_effects=True, vmem_limit_bytes=56 * 1024 * 1024
        ),
        name="superpose",
    )(x, rotations, inverse_cov)


def solution(mesh):
    placed = (P("col", None, "row"), P(), P("row", "col"))
    return jax.shard_map(
        per_device,
        mesh=mesh,
        in_specs=placed,
        out_specs=(P("row", "col"), P(None, None, "col")),
        check_vma=False,
    )
```

```python
import functools

import jax
import jax.numpy as jnp
from jax import lax
from jax.experimental import pallas as pl
from jax.experimental.pallas import tpu as pltpu
from jax.sharding import PartitionSpec as P

POLAR = 12
ROWS = 32
COLS = 8
FB = 32
SUB = 4
ATOMS_LOCAL = 384
FRAMES = ROWS * COLS
MESH = pl.DeviceIdType.MESH
F32 = jnp.float32
BF16 = jnp.bfloat16


def split3(value):
    high = value.astype(BF16)
    rest = value - high.astype(F32)
    middle = rest.astype(BF16)
    low = (rest - middle.astype(F32)).astype(BF16)
    return high, middle, low


def contract(left, right, dims):
    return lax.dot_general(left, right, (dims, ((), ())), preferred_element_type=F32)


def remote(src, dst, send, recv, row, col):
    return pltpu.make_async_remote_copy(
        src_ref=src, dst_ref=dst, send_sem=send, recv_sem=recv, device_id=(row, col), device_id_type=MESH
    )


def polar_all(fit):
    total = jnp.zeros_like(fit[0][0])
    for k in range(3):
        for l in range(3):
            total = total + fit[k][l] * fit[k][l]
    scaling = jnp.sqrt(1.0 + total)
    cur = [[fit[k][i] / scaling for k in range(3)] for i in range(3)]
    for _ in range(POLAR):
        square = [[None] * 3 for _ in range(3)]
        for i in range(3):
            for k in range(i, 3):
                value = cur[i][0] * cur[k][0] + cur[i][1] * cur[k][1] + cur[i][2] * cur[k][2]
                square[i][k] = value
                square[k][i] = value
        nxt = [[None] * 3 for _ in range(3)]
        for i in range(3):
            for l in range(3):
                cubed = square[i][0] * cur[0][l] + square[i][1] * cur[1][l] + square[i][2] * cur[2][l]
                nxt[i][l] = 1.5 * cur[i][l] - 0.5 * cubed
        cur = nxt
    return cur


def kernel(
    x_hbm, rot_hbm, w_hbm, dev_rows, dev_cols, tr_ref,
    rot, wv, cpart, cbuf, csend, cring, csum, hsend, hbuf, asend, abuf, bsend, bbuf, turn, rbuf, ybuf, pbuf, acc, coef, wide, dev_q,
    in_sem, c_send, c_recv, d_send, d_recv, h_send, h_recv, a_send, a_recv, b_send, b_recv, r_send, r_recv, z_send, z_recv,
    y_send, y_recv, x_send, x_recv, s_send, s_recv,
):
    row = lax.axis_index("row")
    col = lax.axis_index("col")
    core = row % 2
    sibling = row + 1 - 2 * core
    y, zl = row // 8, lax.rem(row // 2, 4)
    x, zh = col // 2, lax.rem(col, 2)
    half = zl // 2
    in_half = half == zh

    def dev(x, y, zh, zl):
        return (lax.rem(y, 4) * 4 + lax.rem(zl, 4)) * 2 + core, lax.rem(x, 4) * 2 + zh

    x_ref = rbuf.at[col]
    x_load = pltpu.make_async_copy(x_hbm, x_ref, in_sem.at[0])
    rot_load = pltpu.make_async_copy(rot_hbm, rot, in_sem.at[1])
    w_load = pltpu.make_async_copy(w_hbm, wv, in_sem.at[2])
    x_load.start()
    rot_load.start()
    w_load.start()

    z = 4 * zh + zl

    def plane_peer(m):
        return dev(x + m // 4, y + m % 4, zh, zl)

    def ring_peer(m):
        there = lax.rem(z + m, 8)
        return dev(x, y, there // 4, there)

    barrier = pltpu.get_barrier_semaphore()

    def greet(r, c):
        pl.semaphore_signal(barrier, inc=1, device_id=(r, c), device_id_type=MESH)

    for m in range(1, 16):
        greet(*plane_peer(m))
    for m in range(1, 8):
        greet(*ring_peer(m))
    greet(sibling, col)

    x_load.wait()
    rot_load.wait()
    part = jnp.zeros((3, ATOMS_LOCAL), F32)
    for l in range(3):
        whole = rot[:, l, :]
        mine = jnp.zeros((3, FB), F32)
        for i in range(COLS):
            mine = mine + jnp.where(col == i, whole[:, i * FB : (i + 1) * FB], 0.0)
        block = x_ref[l * FB : (l + 1) * FB, :]
        for piece in split3(mine):
            part = part + contract(piece, block, ((1,), (0,)))
    for l in range(3):
        cpart[0:1, l * ATOMS_LOCAL : (l + 1) * ATOMS_LOCAL] = part[l : l + 1, :]

    @pl.when(x == y)
    def _():
        cbuf[x] = cpart[...]

    @pl.when(in_half)
    def _():
        ybuf[y, 2 * (zl % 2) + zh] = x_ref[...]

    pl.semaphore_wait(barrier, 23)

    def z_copy(i):
        return remote(x_ref, ybuf.at[y, 2 * (zl % 2) + zh], z_send.at[i], z_recv.at[zl % 2, zh], *dev(x, y, half, zl + i))

    def pair_copy():
        return remote(x_ref, rbuf.at[col], z_send.at[0], r_recv.at[col], *dev(x, y, 1 - zh, zl))

    def row_copy(i, other):
        slot = 2 * x + (1 - zh if other else zh)
        source = rbuf.at[slot] if other else x_ref
        return remote(source, rbuf.at[slot], r_send.at[int(other), i], r_recv.at[slot], *dev(x + i, y, zh, zl))

    def y_copy(i, k):
        return remote(ybuf.at[y, k], ybuf.at[y, k], y_send.at[i, k], y_recv.at[y, k], *dev(x, y + i, zh, zl))

    def x_copy(i, k):
        there = lax.rem(x + i, 4)
        return remote(ybuf.at[there, k], pbuf.at[core, k, x], x_send.at[i, k], x_recv.at[k, x], *dev(there, y, zh, zl))

    def share_copy(k):
        return remote(pbuf.at[core, k], pbuf.at[core, k], s_send.at[k], s_recv.at[k], sibling, col)

    def chunk(n):
        odd = lax.rem(zl, 2)
        near = jnp.where(in_half, odd, 1 - odd)
        turn_at = (True, False, in_half, jnp.logical_not(in_half))[n]
        j = near if n == 0 else 1 - near if n == 1 else jnp.where(turn_at, near, 1 - near)
        h = jnp.where(in_half, zh, odd)
        return 2 * j + (h if n < 2 else 1 - h)

    def y_step(n):
        k = chunk(n)

        def forward():
            for i in range(1, 4):
                y_copy(i, k).start()

        def await_z():
            remote(x_ref, ybuf.at[y, k], z_send.at[0], z_recv.at[k // 2, lax.rem(k, 2)], row, col).wait_recv()

        if n % 2:
            await_z()
            forward()
        else:

            @pl.when(jnp.logical_not(in_half))
            def _():
                await_z()
                forward()

            if n:

                @pl.when(in_half)
                def _():
                    forward()

    def x_step(n):
        k = chunk(n)
        for i in range(1, 4):
            there = lax.rem(x + i, 4)

            @pl.when(there != y)
            def _():
                remote(x_ref, ybuf.at[there, k], y_send.at[0, 0], y_recv.at[there, k], row, col).wait_recv()

            x_copy(i, k).start()

        @pl.when(x != y)
        def _():
            remote(x_ref, ybuf.at[x, k], y_send.at[0, 0], y_recv.at[x, k], row, col).wait_recv()

        pbuf[core, k, x] = ybuf[x, k]

    def share_step(n):
        k = chunk(n)
        for i in range(1, 4):
            there = lax.rem(x + i, 4)
            remote(x_ref, pbuf.at[core, k, there], x_send.at[0, 0], x_recv.at[k, there], row, col).wait_recv()
        share_copy(k).start()

    def centre_copy(i):
        return remote(cpart, cbuf.at[x], c_send.at[i], c_recv.at[x], *dev(y, y + i, zh, zl))

    def ring_part_copy(i):
        slot = 2 * lax.rem(zl, 2) + zh
        return remote(csend, cring.at[slot], d_send.at[i], d_recv.at[slot], *dev(x, y, half, zl + i))

    for i in range(4):
        if i:
            centre_copy(i).start()
        else:

            @pl.when(x != y)
            def _():
                centre_copy(0).start()

    pair_copy().start()
    for i in range(1, 4):
        z_copy(i).start()
    for i in range(1, 4):
        row_copy(i, False).start()

    @pl.when(in_half)
    def _():
        for i in range(1, 4):
            y_copy(i, 2 * (zl % 2) + zh).start()

    for p in range(4):

        @pl.when(jnp.logical_or(p != x, x != y))
        def _():
            remote(cpart, cbuf.at[p], c_send.at[0], c_recv.at[p], row, col).wait_recv()

    csend[...] = (cbuf[0] + cbuf[1]) + (cbuf[2] + cbuf[3])
    for i in range(4):
        if i:
            ring_part_copy(i).start()
        else:

            @pl.when(jnp.logical_not(in_half))
            def _():
                ring_part_copy(0).start()

    @pl.when(in_half)
    def _():
        cring[2 * lax.rem(zl, 2) + zh] = csend[...]

    other_slot = 2 * x + 1 - zh
    remote(x_ref, rbuf.at[other_slot], z_send.at[0], r_recv.at[other_slot], row, col).wait_recv()
    for i in range(1, 4):
        row_copy(i, True).start()

    @pl.when(in_half)
    def _():
        ybuf[y, 2 * (zl % 2) + 1 - zh] = rbuf[other_slot]


    y_step(0)
    y_step(1)
    y_step(2)
    for j in range(2):
        for h in range(2):

            @pl.when(jnp.logical_or(jnp.logical_not(in_half), jnp.logical_or(lax.rem(zl, 2) != j, zh != h)))
            def _():
                remote(csend, cring.at[2 * j + h], d_send.at[0], d_recv.at[2 * j + h], row, col).wait_recv()

        csum[core, j] = (cring[2 * j] + cring[2 * j + 1]) * (1.0 / FRAMES)

    def half_copy(i, src, dst):
        return remote(src, dst, h_send.at[i], h_recv.at[i], sibling, col)

    centre_half = half_copy(0, csum.at[core], csum.at[core])
    centre_half.start()
    half_copy(0, csum.at[core], csum.at[1 - core]).wait_recv()

    w_load.wait()
    lanes = [[csum[q % 2, q // 2, :, l * ATOMS_LOCAL : (l + 1) * ATOMS_LOCAL] for q in range(SUB)] for l in range(3)]

    def weigh(i, carry):
        start = pl.multiple_of(i * 32, 32)
        sums = [jnp.zeros((32, 128), F32) for _ in range(3)]
        for q in range(SUB):
            for t in range(3):
                tile = wv[pl.ds(start, 32), q * 384 + t * 128 : q * 384 + (t + 1) * 128]
                for l in range(3):
                    sums[l] = sums[l] + tile * lanes[l][q][:, t * 128 : (t + 1) * 128]
        for l in range(3):
            for p, piece in enumerate(split3(sums[l])):
                acc[pl.ds(start, 32), (3 * l + p) * 128 : (3 * l + p + 1) * 128] = piece
        return carry

    lax.fori_loop(0, 12, weigh, 0)
    shape = (8, 9 * 128)
    owner_of = lax.broadcasted_iota(jnp.int32, shape, 1) // 384
    chooser = jnp.where(owner_of == lax.broadcasted_iota(jnp.int32, shape, 0), 1.0, 0.0).astype(BF16)
    weighted = contract(chooser, acc[...], ((1,), (1,)))

    y_step(3)
    for i in range(1, 4):
        for h in range(2):
            slot = 2 * lax.rem(x + i, 4) + h
            remote(x_ref, rbuf.at[slot], r_send.at[0, 0], r_recv.at[slot], row, col).wait_recv()
    pieces = jnp.concatenate(split3(weighted), axis=0)
    first = core == 0
    for k in range(3):
        frames_k = rbuf[:, k * FB : (k + 1) * FB, :].reshape(FRAMES, ATOMS_LOCAL)
        product = contract(pieces, frames_k, ((1,), (1,)))
        product = product[0:8] + product[8:16] + product[16:24]
        own = jnp.where(first, product[:, 0:128], product[:, 128:256])
        others = jnp.where(first, product[:, 128:256], product[:, 0:128])
        for l in range(3):
            at = (3 * k + l) * 128
            asend[0:1, at : at + 128] = own[l : l + 1, :]
            hsend[0:1, at : at + 128] = others[l : l + 1, :]
    fit_half = half_copy(1, hsend, hbuf.at[0])
    fit_half.start()
    x_step(0)
    fit_half.wait_recv()
    asend[...] = asend[...] + hbuf[0]
    a_slot = 4 * x + y
    abuf[a_slot] = asend[...]

    def plane_copy(m):
        return remote(asend, abuf.at[a_slot], a_send.at[m], a_recv.at[a_slot], *plane_peer(m))

    def ring_copy(m):
        return remote(bsend, bbuf.at[z], b_send.at[m], b_recv.at[z], *ring_peer(m))

    for m in range(1, 16):
        plane_copy(m).start()
    x_step(1)
    x_step(2)
    for m in range(1, 16):
        slot = 4 * lax.rem(x + m // 4, 4) + lax.rem(y + m % 4, 4)
        remote(asend, abuf.at[slot], a_send.at[0], a_recv.at[slot], row, col).wait_recv()
    bsend[...] = jnp.sum(abuf[...], axis=0)
    bbuf[z] = bsend[...]
    for m in range(1, 8):
        ring_copy(m).start()

    x_step(3)
    share_step(0)
    share_step(1)
    centre_rows = jnp.zeros((8, ATOMS_LOCAL), F32)
    for l in range(3):
        frames_l = rbuf[:, l * FB : (l + 1) * FB, :].reshape(FRAMES, ATOMS_LOCAL)
        spin = jnp.concatenate([rot[:, l, :], jnp.zeros((5, FRAMES), F32)], axis=0)
        product = contract(jnp.concatenate(split3(spin), axis=0), frames_l, ((1,), (0,)))
        centre_rows = centre_rows + (product[0:8] + product[8:16] + product[16:24])
    centre_rows = centre_rows * (1.0 / FRAMES)

    for m in range(1, 8):
        slot = lax.rem(z + m, 8)
        remote(bsend, bbuf.at[slot], b_send.at[0], b_recv.at[slot], row, col).wait_recv()
    fitted = jnp.sum(bbuf[...], axis=0)

    turned = polar_all([[fitted[:, (3 * k + l) * 128 : (3 * k + l + 1) * 128] for l in range(3)] for k in range(3)])
    for k in range(3):
        for l in range(3):
            turn[core, :, (3 * k + l) * 128 : (3 * k + l + 1) * 128] = turned[k][l]
    turn_half = half_copy(2, turn.at[core], turn.at[core])
    turn_half.start()
    share_step(2)
    half_copy(2, turn.at[core], turn.at[1 - core]).wait_recv()
    picked = jnp.where(col < 4, turn[0], turn[1])
    quarter = lax.rem(col, 4)
    for k in range(3):
        for l in range(3):
            line = picked[:, (3 * k + l) * 128 : (3 * k + l + 1) * 128]
            mine = jnp.zeros((1, FB), F32)
            for i in range(4):
                mine = mine + jnp.where(quarter == i, line[:, i * FB : (i + 1) * FB], 0.0)
            tr_ref[k, l : l + 1, :] = mine
    for half_of in range(2):
        for j in range(9):
            coef[j : j + 1, :] = turn[half_of, :, j * 128 : (j + 1) * 128]
        upright = jnp.transpose(coef[...])
        for c in range(4):
            for j in range(9):
                wide[j, 4 * half_of + c] = jnp.broadcast_to(upright[c * FB : (c + 1) * FB, j : j + 1], (FB, 128))

    def deviate(target, count, block_of, start_of, centre):
        base = [jnp.broadcast_to(centre[k], (FB, ATOMS_LOCAL)) for k in range(3)]

        def body(i, carry):
            block = block_of(i).astype(F32)
            xs = [block[l * FB : (l + 1) * FB, :] for l in range(3)]
            c = start_of(i)
            values = []
            for k in range(3):
                terms = []
                for l in range(3):
                    factor = wide[3 * k + l, c]
                    terms.append(jnp.concatenate([factor, factor, factor], axis=1) * xs[l])
                values.append((terms[0] + terms[1]) + terms[2] - base[k])
            target[pl.ds(pl.multiple_of(c * 96, 96), 96), :] = jnp.concatenate(values, axis=0).astype(BF16)
            return carry

        lax.fori_loop(0, count, body, 0)

    def deviate_piece(owner, n):
        k = chunk(n)
        j = k // 2
        centre = [csum[owner, j, :, i * ATOMS_LOCAL : (i + 1) * ATOMS_LOCAL] for i in range(3)]
        deviate(
            dev_cols.at[2 * j + owner], 4, lambda i: pbuf[owner, k, i], lambda i: 2 * i + lax.rem(k, 2), centre
        )

    def shared_wait(n):
        k = chunk(n)
        remote(pbuf.at[1 - core, k], pbuf.at[1 - core, k], s_send.at[0], s_recv.at[k], row, col).wait_recv()

    deviate(dev_q, COLS, lambda i: rbuf[i], lambda i: i, [centre_rows[k : k + 1, :] for k in range(3)])
    dev_rows[...] = jnp.transpose(dev_q[...])
    share_step(3)
    for n in range(3):
        deviate_piece(core, n)
    for n in range(3):
        shared_wait(n)
        deviate_piece(1 - core, n)
    deviate_piece(core, 3)
    shared_wait(3)
    deviate_piece(1 - core, 3)

    for i in range(4):
        if i:
            centre_copy(i).wait_send()
            ring_part_copy(i).wait_send()
        else:

            @pl.when(x != y)
            def _():
                centre_copy(0).wait_send()

            @pl.when(jnp.logical_not(in_half))
            def _():
                ring_part_copy(0).wait_send()

    for m in range(1, 16):
        plane_copy(m).wait_send()
    for m in range(1, 8):
        ring_copy(m).wait_send()
    centre_half.wait_send()
    fit_half.wait_send()
    turn_half.wait_send()
    pair_copy().wait_send()
    for i in range(1, 4):
        z_copy(i).wait_send()
        row_copy(i, False).wait_send()
        row_copy(i, True).wait_send()
        for k in range(4):
            y_copy(i, k).wait_send()
            x_copy(i, k).wait_send()
    for k in range(4):
        share_copy(k).wait_send()


def multiply(rows_ref, cols_ref, tr_ref, cov_ref, out_ref):
    q = pl.program_id(0)
    out_ref[...] = tr_ref[...]
    cov_ref[...] = contract(rows_ref[...], cols_ref[q], ((1,), (0,))) * (1.0 / (3 * FRAMES))


def per_device(frames, rotations, inverse_cov):
    x = jnp.transpose(frames, (1, 0, 2)).reshape(96, ATOMS_LOCAL)
    dma = pltpu.SemaphoreType.DMA
    vmem = pl.BlockSpec(memory_space=pltpu.VMEM)
    hbm = pl.BlockSpec(memory_space=pltpu.HBM)
    operands = [pltpu.with_memory_space_constraint(value, pltpu.HBM) for value in (x, rotations, inverse_cov)]
    dev_rows, dev_cols, turned = pl.pallas_call(
        kernel,
        out_shape=(
            jax.ShapeDtypeStruct((ATOMS_LOCAL, 3 * FRAMES), BF16),
            jax.ShapeDtypeStruct((SUB, 3 * FRAMES, ATOMS_LOCAL), BF16),
            jax.ShapeDtypeStruct((3, 3, FB), F32),
        ),
        in_specs=[hbm, hbm, hbm],
        out_specs=(vmem, vmem, vmem),
        scratch_shapes=[
            pltpu.VMEM((3, 3, 256), F32),
            pltpu.VMEM((384, 1536), F32),
            pltpu.VMEM((1, 1152), F32),
            pltpu.VMEM((4, 1, 1152), F32),
            pltpu.VMEM((1, 1152), F32),
            pltpu.VMEM((4, 1, 1152), F32),
            pltpu.VMEM((2, 2, 1, 1152), F32),
            pltpu.VMEM((1, 1152), F32),
            pltpu.VMEM((1, 1, 1152), F32),
            pltpu.VMEM((1, 1152), F32),
            pltpu.VMEM((16, 1, 1152), F32),
            pltpu.VMEM((1, 1152), F32),
            pltpu.VMEM((8, 1, 1152), F32),
            pltpu.VMEM((2, 1, 1152), F32),
            pltpu.VMEM((8, 96, 384), BF16),
            pltpu.VMEM((4, 4, 96, 384), BF16),
            pltpu.VMEM((2, 4, 4, 96, 384), BF16),
            pltpu.VMEM((384, 1152), BF16),
            pltpu.VMEM((16, 128), F32),
            pltpu.VMEM((9, 8, 32, 128), F32),
            pltpu.VMEM((768, 384), BF16),
            dma((3,)),
            dma((4,)), dma((4,)),
            dma((4,)), dma((4,)),
            dma((3,)), dma((3,)),
            dma((16,)), dma((16,)),
            dma((8,)), dma((8,)),
            dma((2, 4)), dma((8,)),
            dma((4,)), dma((2, 2)),
            dma((4, 4)), dma((4, 4)),
            dma((4, 4)), dma((4, 4)),
            dma((4,)), dma((4,)),
        ],
        compiler_params=pltpu.CompilerParams(
            collective_id=0, has_side_effects=True, vmem_limit_bytes=32 * 1024 * 1024
        ),
        name="superpose",
    )(*operands)
    return pl.pallas_call(
        multiply,
        grid=(SUB,),
        out_shape=(
            jax.ShapeDtypeStruct((ATOMS_LOCAL, SUB * ATOMS_LOCAL), F32),
            jax.ShapeDtypeStruct((3, 3, FB), F32),
        ),
        in_specs=[vmem, vmem, vmem],
        out_specs=(
            pl.BlockSpec((ATOMS_LOCAL, ATOMS_LOCAL), lambda q: (0, q)),
            pl.BlockSpec((3, 3, FB), lambda q: (0, 0, 0)),
        ),
        compiler_params=pltpu.CompilerParams(
            dimension_semantics=("arbitrary",), vmem_limit_bytes=16 * 1024 * 1024
        ),
        name="covariance",
    )(dev_rows, dev_cols, turned)


def solution(mesh):
    placed = (P("col", None, "row"), P(), P("row", "col"))
    return jax.shard_map(
        per_device,
        mesh=mesh,
        in_specs=placed,
        out_specs=(P("row", "col"), P(None, None, "col")),
        check_vma=False,
    )
```

```python
import functools

import jax
import jax.numpy as jnp
from jax import lax
from jax.experimental import pallas as pl
from jax.experimental.pallas import tpu as pltpu
from jax.sharding import PartitionSpec as P

POLAR = 12
ROWS = 32
COLS = 8
FB = 32
SUB = 4
ATOMS_LOCAL = 384
FRAMES = ROWS * COLS
MESH = pl.DeviceIdType.MESH
F32 = jnp.float32
BF16 = jnp.bfloat16


def split3(value):
    high = value.astype(BF16)
    rest = value - high.astype(F32)
    middle = rest.astype(BF16)
    low = (rest - middle.astype(F32)).astype(BF16)
    return high, middle, low


def contract(left, right, dims):
    return lax.dot_general(left, right, (dims, ((), ())), preferred_element_type=F32)


def remote(src, dst, send, recv, row, col):
    return pltpu.make_async_remote_copy(
        src_ref=src, dst_ref=dst, send_sem=send, recv_sem=recv, device_id=(row, col), device_id_type=MESH
    )


def polar_all(fit):
    total = jnp.zeros_like(fit[0][0])
    for k in range(3):
        for l in range(3):
            total = total + fit[k][l] * fit[k][l]
    scaling = jnp.sqrt(1.0 + total)
    cur = [[fit[k][i] / scaling for k in range(3)] for i in range(3)]
    for _ in range(POLAR):
        square = [[None] * 3 for _ in range(3)]
        for i in range(3):
            for k in range(i, 3):
                value = cur[i][0] * cur[k][0] + cur[i][1] * cur[k][1] + cur[i][2] * cur[k][2]
                square[i][k] = value
                square[k][i] = value
        nxt = [[None] * 3 for _ in range(3)]
        for i in range(3):
            for l in range(3):
                cubed = square[i][0] * cur[0][l] + square[i][1] * cur[1][l] + square[i][2] * cur[2][l]
                nxt[i][l] = 1.5 * cur[i][l] - 0.5 * cubed
        cur = nxt
    return cur


def kernel(
    x_hbm, rot_hbm, w_hbm, dev_rows, dev_cols, tr_ref,
    rot, wv, cpart, cbuf, csend, cring, csum, hsend, hbuf, asend, abuf, bsend, bbuf, turn, rbuf, ybuf, pbuf, acc, coef, wide, dev_q,
    in_sem, c_send, c_recv, d_send, d_recv, h_send, h_recv, a_send, a_recv, b_send, b_recv, r_send, r_recv, z_send, z_recv,
    pair_send,
    y_send, y_recv, x_send, x_recv, s_send, s_recv,
):
    row = lax.axis_index("row")
    col = lax.axis_index("col")
    core = row % 2
    sibling = row + 1 - 2 * core
    y, zl = row // 8, lax.rem(row // 2, 4)
    x, zh = col // 2, lax.rem(col, 2)
    half = zl // 2
    in_half = half == zh

    def dev(x, y, zh, zl):
        return (lax.rem(y, 4) * 4 + lax.rem(zl, 4)) * 2 + core, lax.rem(x, 4) * 2 + zh

    x_ref = rbuf.at[col]
    x_load = pltpu.make_async_copy(x_hbm, x_ref, in_sem.at[0])
    rot_load = pltpu.make_async_copy(rot_hbm, rot, in_sem.at[1])
    w_load = pltpu.make_async_copy(w_hbm, wv, in_sem.at[2])
    x_load.start()
    rot_load.start()
    w_load.start()

    z = 4 * zh + zl

    def plane_peer(m):
        return dev(x + m // 4, y + m % 4, zh, zl)

    def ring_peer(m):
        there = lax.rem(z + m, 8)
        return dev(x, y, there // 4, there)

    barrier = pltpu.get_barrier_semaphore()

    def greet(r, c):
        pl.semaphore_signal(barrier, inc=1, device_id=(r, c), device_id_type=MESH)

    for m in range(1, 16):
        greet(*plane_peer(m))
    for m in range(1, 8):
        greet(*ring_peer(m))
    greet(sibling, col)

    x_load.wait()
    rot_load.wait()
    part = jnp.zeros((3, ATOMS_LOCAL), F32)
    for l in range(3):
        whole = rot[:, l, :]
        mine = jnp.zeros((3, FB), F32)
        for i in range(COLS):
            mine = mine + jnp.where(col == i, whole[:, i * FB : (i + 1) * FB], 0.0)
        block = x_ref[l * FB : (l + 1) * FB, :]
        for piece in split3(mine):
            part = part + contract(piece, block, ((1,), (0,)))
    for l in range(3):
        cpart[0:1, l * ATOMS_LOCAL : (l + 1) * ATOMS_LOCAL] = part[l : l + 1, :]

    @pl.when(x == y)
    def _():
        cbuf[x] = cpart[...]

    @pl.when(in_half)
    def _():
        ybuf[y, 2 * (zl % 2) + zh] = x_ref[...]

    pl.semaphore_wait(barrier, 23)

    def any_of(*places):
        found = z == places[0]
        for value in places[1:]:
            found = jnp.logical_or(found, z == value)
        return found

    steps = ((1, any_of(0, 1, 3, 6)), (-1, any_of(1, 4, 6, 7)), (2, any_of(1, 3)), (-2, any_of(4, 6)))

    def z_copy(m, other):
        there = lax.rem(z + 8 + steps[m][0], 8)
        h = 1 - zh if other else zh
        return remote(
            rbuf.at[2 * x + h], ybuf.at[y, 2 * lax.rem(zl, 2) + h], z_send.at[m, int(other)],
            z_recv.at[lax.rem(zl, 2), h], *dev(x, y, there // 4, there),
        )

    def for_z(other, action):
        for m in range(4):

            @pl.when(steps[m][1])
            def _():
                action(z_copy(m, other))

    def pair_copy():
        return remote(x_ref, rbuf.at[col], pair_send, r_recv.at[col], *dev(x, y, 1 - zh, zl))

    def row_copy(i, other):
        slot = 2 * x + (1 - zh if other else zh)
        source = rbuf.at[slot] if other else x_ref
        return remote(source, rbuf.at[slot], r_send.at[int(other), i], r_recv.at[slot], *dev(x + i, y, zh, zl))

    def y_copy(i, k):
        return remote(ybuf.at[y, k], ybuf.at[y, k], y_send.at[i, k], y_recv.at[y, k], *dev(x, y + i, zh, zl))

    def x_copy(i, k):
        there = lax.rem(x + i, 4)
        return remote(ybuf.at[there, k], pbuf.at[core, k, x], x_send.at[i, k], x_recv.at[k, x], *dev(there, y, zh, zl))

    def share_copy(k):
        return remote(pbuf.at[core, k], pbuf.at[core, k], s_send.at[k], s_recv.at[k], sibling, col)

    def chunk(n):
        odd = lax.rem(zl, 2)
        j = odd if n % 2 == 0 else 1 - odd
        h = zh if n < 2 else 1 - zh
        return jnp.where(in_half, 2 * j + h, (2, 1, 3, 0)[n])

    def y_step(n):
        k = chunk(n)

        def forward():
            for i in range(1, 4):
                y_copy(i, k).start()

        def await_z():
            remote(x_ref, ybuf.at[y, k], pair_send, z_recv.at[k // 2, lax.rem(k, 2)], row, col).wait_recv()

        if n % 2:
            await_z()
            forward()
        else:

            @pl.when(jnp.logical_not(in_half))
            def _():
                await_z()
                forward()

            if n:

                @pl.when(in_half)
                def _():
                    forward()

    def x_step(n):
        k = chunk(n)
        for i in range(1, 4):
            there = lax.rem(x + i, 4)

            @pl.when(there != y)
            def _():
                remote(x_ref, ybuf.at[there, k], y_send.at[0, 0], y_recv.at[there, k], row, col).wait_recv()

            x_copy(i, k).start()

        @pl.when(x != y)
        def _():
            remote(x_ref, ybuf.at[x, k], y_send.at[0, 0], y_recv.at[x, k], row, col).wait_recv()

        pbuf[core, k, x] = ybuf[x, k]

    def share_step(n):
        k = chunk(n)
        for i in range(1, 4):
            there = lax.rem(x + i, 4)
            remote(x_ref, pbuf.at[core, k, there], x_send.at[0, 0], x_recv.at[k, there], row, col).wait_recv()
        share_copy(k).start()

    def centre_copy(i):
        return remote(cpart, cbuf.at[x], c_send.at[i], c_recv.at[x], *dev(y, y + i, zh, zl))

    def ring_part_copy(i):
        slot = 2 * lax.rem(zl, 2) + zh
        return remote(csend, cring.at[slot], d_send.at[i], d_recv.at[slot], *dev(x, y, half, zl + i))

    for i in range(4):
        if i:
            centre_copy(i).start()
        else:

            @pl.when(x != y)
            def _():
                centre_copy(0).start()

    pair_copy().start()
    for_z(False, lambda copy: copy.start())
    for i in range(1, 4):
        row_copy(i, False).start()

    @pl.when(in_half)
    def _():
        for i in range(1, 4):
            y_copy(i, 2 * (zl % 2) + zh).start()

    for p in range(4):

        @pl.when(jnp.logical_or(p != x, x != y))
        def _():
            remote(cpart, cbuf.at[p], c_send.at[0], c_recv.at[p], row, col).wait_recv()

    csend[...] = (cbuf[0] + cbuf[1]) + (cbuf[2] + cbuf[3])
    for i in range(4):
        if i:
            ring_part_copy(i).start()
        else:

            @pl.when(jnp.logical_not(in_half))
            def _():
                ring_part_copy(0).start()

    @pl.when(in_half)
    def _():
        cring[2 * lax.rem(zl, 2) + zh] = csend[...]

    other_slot = 2 * x + 1 - zh
    remote(x_ref, rbuf.at[other_slot], pair_send, r_recv.at[other_slot], row, col).wait_recv()
    for_z(True, lambda copy: copy.start())
    for i in range(1, 4):
        row_copy(i, True).start()

    @pl.when(in_half)
    def _():
        ybuf[y, 2 * (zl % 2) + 1 - zh] = rbuf[other_slot]


    y_step(0)
    y_step(1)
    y_step(2)
    for j in range(2):
        for h in range(2):

            @pl.when(jnp.logical_or(jnp.logical_not(in_half), jnp.logical_or(lax.rem(zl, 2) != j, zh != h)))
            def _():
                remote(csend, cring.at[2 * j + h], d_send.at[0], d_recv.at[2 * j + h], row, col).wait_recv()

        csum[core, j] = (cring[2 * j] + cring[2 * j + 1]) * (1.0 / FRAMES)

    def half_copy(i, src, dst):
        return remote(src, dst, h_send.at[i], h_recv.at[i], sibling, col)

    centre_half = half_copy(0, csum.at[core], csum.at[core])
    centre_half.start()
    half_copy(0, csum.at[core], csum.at[1 - core]).wait_recv()

    x_step(0)
    w_load.wait()
    lanes = [[csum[q % 2, q // 2, :, l * ATOMS_LOCAL : (l + 1) * ATOMS_LOCAL] for q in range(SUB)] for l in range(3)]

    def weigh(i, carry):
        start = pl.multiple_of(i * 32, 32)
        sums = [jnp.zeros((32, 128), F32) for _ in range(3)]
        for q in range(SUB):
            for t in range(3):
                tile = wv[pl.ds(start, 32), q * 384 + t * 128 : q * 384 + (t + 1) * 128]
                for l in range(3):
                    sums[l] = sums[l] + tile * lanes[l][q][:, t * 128 : (t + 1) * 128]
        for l in range(3):
            for p, piece in enumerate(split3(sums[l])):
                acc[pl.ds(start, 32), (3 * l + p) * 128 : (3 * l + p + 1) * 128] = piece
        return carry

    lax.fori_loop(0, 12, weigh, 0)
    shape = (8, 9 * 128)
    owner_of = lax.broadcasted_iota(jnp.int32, shape, 1) // 384
    chooser = jnp.where(owner_of == lax.broadcasted_iota(jnp.int32, shape, 0), 1.0, 0.0).astype(BF16)
    weighted = contract(chooser, acc[...], ((1,), (1,)))

    for i in range(1, 4):
        for h in range(2):
            slot = 2 * lax.rem(x + i, 4) + h
            remote(x_ref, rbuf.at[slot], r_send.at[0, 0], r_recv.at[slot], row, col).wait_recv()
    pieces = jnp.concatenate(split3(weighted), axis=0)
    first = core == 0
    for k in range(3):
        frames_k = rbuf[:, k * FB : (k + 1) * FB, :].reshape(FRAMES, ATOMS_LOCAL)
        product = contract(pieces, frames_k, ((1,), (1,)))
        product = product[0:8] + product[8:16] + product[16:24]
        own = jnp.where(first, product[:, 0:128], product[:, 128:256])
        others = jnp.where(first, product[:, 128:256], product[:, 0:128])
        for l in range(3):
            at = (3 * k + l) * 128
            asend[0:1, at : at + 128] = own[l : l + 1, :]
            hsend[0:1, at : at + 128] = others[l : l + 1, :]
    fit_half = half_copy(1, hsend, hbuf.at[0])
    fit_half.start()
    fit_half.wait_recv()
    asend[...] = asend[...] + hbuf[0]
    a_slot = 4 * x + y
    abuf[a_slot] = asend[...]

    def plane_copy(m):
        return remote(asend, abuf.at[a_slot], a_send.at[m], a_recv.at[a_slot], *plane_peer(m))

    def ring_copy(m):
        return remote(bsend, bbuf.at[z], b_send.at[m], b_recv.at[z], *ring_peer(m))

    for m in range(1, 16):
        plane_copy(m).start()
    y_step(3)
    x_step(1)
    x_step(2)
    for m in range(1, 16):
        slot = 4 * lax.rem(x + m // 4, 4) + lax.rem(y + m % 4, 4)
        remote(asend, abuf.at[slot], a_send.at[0], a_recv.at[slot], row, col).wait_recv()
    bsend[...] = jnp.sum(abuf[...], axis=0)
    bbuf[z] = bsend[...]
    for m in range(1, 8):
        ring_copy(m).start()

    x_step(3)
    share_step(0)
    share_step(1)
    centre_rows = jnp.zeros((8, ATOMS_LOCAL), F32)
    for l in range(3):
        frames_l = rbuf[:, l * FB : (l + 1) * FB, :].reshape(FRAMES, ATOMS_LOCAL)
        spin = jnp.concatenate([rot[:, l, :], jnp.zeros((5, FRAMES), F32)], axis=0)
        product = contract(jnp.concatenate(split3(spin), axis=0), frames_l, ((1,), (0,)))
        centre_rows = centre_rows + (product[0:8] + product[8:16] + product[16:24])
    centre_rows = centre_rows * (1.0 / FRAMES)

    for m in range(1, 8):
        slot = lax.rem(z + m, 8)
        remote(bsend, bbuf.at[slot], b_send.at[0], b_recv.at[slot], row, col).wait_recv()
    fitted = jnp.sum(bbuf[...], axis=0)

    turned = polar_all([[fitted[:, (3 * k + l) * 128 : (3 * k + l + 1) * 128] for l in range(3)] for k in range(3)])
    for k in range(3):
        for l in range(3):
            turn[core, :, (3 * k + l) * 128 : (3 * k + l + 1) * 128] = turned[k][l]
    turn_half = half_copy(2, turn.at[core], turn.at[core])
    turn_half.start()
    share_step(2)
    half_copy(2, turn.at[core], turn.at[1 - core]).wait_recv()
    picked = jnp.where(col < 4, turn[0], turn[1])
    quarter = lax.rem(col, 4)
    for k in range(3):
        for l in range(3):
            line = picked[:, (3 * k + l) * 128 : (3 * k + l + 1) * 128]
            mine = jnp.zeros((1, FB), F32)
            for i in range(4):
                mine = mine + jnp.where(quarter == i, line[:, i * FB : (i + 1) * FB], 0.0)
            tr_ref[k, l : l + 1, :] = mine
    for half_of in range(2):
        for j in range(9):
            coef[j : j + 1, :] = turn[half_of, :, j * 128 : (j + 1) * 128]
        upright = jnp.transpose(coef[...])
        for c in range(4):
            for j in range(9):
                wide[j, 4 * half_of + c] = jnp.broadcast_to(upright[c * FB : (c + 1) * FB, j : j + 1], (FB, 128))

    def deviate(target, count, block_of, start_of, centre):
        base = [jnp.broadcast_to(centre[k], (FB, ATOMS_LOCAL)) for k in range(3)]

        def body(i, carry):
            block = block_of(i).astype(F32)
            xs = [block[l * FB : (l + 1) * FB, :] for l in range(3)]
            c = start_of(i)
            values = []
            for k in range(3):
                terms = []
                for l in range(3):
                    factor = wide[3 * k + l, c]
                    terms.append(jnp.concatenate([factor, factor, factor], axis=1) * xs[l])
                values.append((terms[0] + terms[1]) + terms[2] - base[k])
            target[pl.ds(pl.multiple_of(c * 96, 96), 96), :] = jnp.concatenate(values, axis=0).astype(BF16)
            return carry

        lax.fori_loop(0, count, body, 0)

    def deviate_piece(owner, n):
        k = chunk(n)
        j = k // 2
        centre = [csum[owner, j, :, i * ATOMS_LOCAL : (i + 1) * ATOMS_LOCAL] for i in range(3)]
        deviate(
            dev_cols.at[2 * j + owner], 4, lambda i: pbuf[owner, k, i], lambda i: 2 * i + lax.rem(k, 2), centre
        )

    def shared_wait(n):
        k = chunk(n)
        remote(pbuf.at[1 - core, k], pbuf.at[1 - core, k], s_send.at[0], s_recv.at[k], row, col).wait_recv()

    deviate(dev_q, COLS, lambda i: rbuf[i], lambda i: i, [centre_rows[k : k + 1, :] for k in range(3)])
    dev_rows[...] = jnp.transpose(dev_q[...])
    share_step(3)
    for n in range(3):
        deviate_piece(core, n)
    for n in range(3):
        shared_wait(n)
        deviate_piece(1 - core, n)
    deviate_piece(core, 3)
    shared_wait(3)
    deviate_piece(1 - core, 3)

    for i in range(4):
        if i:
            centre_copy(i).wait_send()
            ring_part_copy(i).wait_send()
        else:

            @pl.when(x != y)
            def _():
                centre_copy(0).wait_send()

            @pl.when(jnp.logical_not(in_half))
            def _():
                ring_part_copy(0).wait_send()

    for m in range(1, 16):
        plane_copy(m).wait_send()
    for m in range(1, 8):
        ring_copy(m).wait_send()
    centre_half.wait_send()
    fit_half.wait_send()
    turn_half.wait_send()
    pair_copy().wait_send()
    for_z(False, lambda copy: copy.wait_send())
    for_z(True, lambda copy: copy.wait_send())
    for i in range(1, 4):
        row_copy(i, False).wait_send()
        row_copy(i, True).wait_send()
        for k in range(4):
            y_copy(i, k).wait_send()
            x_copy(i, k).wait_send()
    for k in range(4):
        share_copy(k).wait_send()


def multiply(rows_ref, cols_ref, tr_ref, cov_ref, out_ref):
    q = pl.program_id(0)
    out_ref[...] = tr_ref[...]
    cov_ref[...] = contract(rows_ref[...], cols_ref[q], ((1,), (0,))) * (1.0 / (3 * FRAMES))


def per_device(frames, rotations, inverse_cov):
    x = jnp.transpose(frames, (1, 0, 2)).reshape(96, ATOMS_LOCAL)
    dma = pltpu.SemaphoreType.DMA
    vmem = pl.BlockSpec(memory_space=pltpu.VMEM)
    hbm = pl.BlockSpec(memory_space=pltpu.HBM)
    operands = [pltpu.with_memory_space_constraint(value, pltpu.HBM) for value in (x, rotations, inverse_cov)]
    dev_rows, dev_cols, turned = pl.pallas_call(
        kernel,
        out_shape=(
            jax.ShapeDtypeStruct((ATOMS_LOCAL, 3 * FRAMES), BF16),
            jax.ShapeDtypeStruct((SUB, 3 * FRAMES, ATOMS_LOCAL), BF16),
            jax.ShapeDtypeStruct((3, 3, FB), F32),
        ),
        in_specs=[hbm, hbm, hbm],
        out_specs=(vmem, vmem, vmem),
        scratch_shapes=[
            pltpu.VMEM((3, 3, 256), F32),
            pltpu.VMEM((384, 1536), F32),
            pltpu.VMEM((1, 1152), F32),
            pltpu.VMEM((4, 1, 1152), F32),
            pltpu.VMEM((1, 1152), F32),
            pltpu.VMEM((4, 1, 1152), F32),
            pltpu.VMEM((2, 2, 1, 1152), F32),
            pltpu.VMEM((1, 1152), F32),
            pltpu.VMEM((1, 1, 1152), F32),
            pltpu.VMEM((1, 1152), F32),
            pltpu.VMEM((16, 1, 1152), F32),
            pltpu.VMEM((1, 1152), F32),
            pltpu.VMEM((8, 1, 1152), F32),
            pltpu.VMEM((2, 1, 1152), F32),
            pltpu.VMEM((8, 96, 384), BF16),
            pltpu.VMEM((4, 4, 96, 384), BF16),
            pltpu.VMEM((2, 4, 4, 96, 384), BF16),
            pltpu.VMEM((384, 1152), BF16),
            pltpu.VMEM((16, 128), F32),
            pltpu.VMEM((9, 8, 32, 128), F32),
            pltpu.VMEM((768, 384), BF16),
            dma((3,)),
            dma((4,)), dma((4,)),
            dma((4,)), dma((4,)),
            dma((3,)), dma((3,)),
            dma((16,)), dma((16,)),
            dma((8,)), dma((8,)),
            dma((2, 4)), dma((8,)),
            dma((4, 2)), dma((2, 2)), dma(()),
            dma((4, 4)), dma((4, 4)),
            dma((4, 4)), dma((4, 4)),
            dma((4,)), dma((4,)),
        ],
        compiler_params=pltpu.CompilerParams(
            collective_id=0, has_side_effects=True, vmem_limit_bytes=32 * 1024 * 1024
        ),
        name="superpose",
    )(*operands)
    return pl.pallas_call(
        multiply,
        grid=(SUB,),
        out_shape=(
            jax.ShapeDtypeStruct((ATOMS_LOCAL, SUB * ATOMS_LOCAL), F32),
            jax.ShapeDtypeStruct((3, 3, FB), F32),
        ),
        in_specs=[vmem, vmem, vmem],
        out_specs=(
            pl.BlockSpec((ATOMS_LOCAL, ATOMS_LOCAL), lambda q: (0, q)),
            pl.BlockSpec((3, 3, FB), lambda q: (0, 0, 0)),
        ),
        compiler_params=pltpu.CompilerParams(
            dimension_semantics=("arbitrary",), vmem_limit_bytes=16 * 1024 * 1024
        ),
        name="covariance",
    )(dev_rows, dev_cols, turned)


def solution(mesh):
    placed = (P("col", None, "row"), P(), P("row", "col"))
    return jax.shard_map(
        per_device,
        mesh=mesh,
        in_specs=placed,
        out_specs=(P("row", "col"), P(None, None, "col")),
        check_vma=False,
    )
```

```python
import functools

import jax
import jax.numpy as jnp
from jax import lax
from jax.experimental import pallas as pl
from jax.experimental.pallas import tpu as pltpu
from jax.sharding import PartitionSpec as P

POLAR = 12
ROWS = 32
COLS = 8
FB = 32
SUB = 4
ATOMS_LOCAL = 384
FRAMES = ROWS * COLS
MESH = pl.DeviceIdType.MESH
F32 = jnp.float32
BF16 = jnp.bfloat16


def split3(value):
    high = value.astype(BF16)
    rest = value - high.astype(F32)
    middle = rest.astype(BF16)
    low = (rest - middle.astype(F32)).astype(BF16)
    return high, middle, low


def contract(left, right, dims):
    return lax.dot_general(left, right, (dims, ((), ())), preferred_element_type=F32)


def remote(src, dst, send, recv, row, col):
    return pltpu.make_async_remote_copy(
        src_ref=src, dst_ref=dst, send_sem=send, recv_sem=recv, device_id=(row, col), device_id_type=MESH
    )


def polar_all(fit):
    total = jnp.zeros_like(fit[0][0])
    for k in range(3):
        for l in range(3):
            total = total + fit[k][l] * fit[k][l]
    scaling = jnp.sqrt(1.0 + total)
    cur = [[fit[k][i] / scaling for k in range(3)] for i in range(3)]
    for _ in range(POLAR):
        square = [[None] * 3 for _ in range(3)]
        for i in range(3):
            for k in range(i, 3):
                value = cur[i][0] * cur[k][0] + cur[i][1] * cur[k][1] + cur[i][2] * cur[k][2]
                square[i][k] = value
                square[k][i] = value
        nxt = [[None] * 3 for _ in range(3)]
        for i in range(3):
            for l in range(3):
                cubed = square[i][0] * cur[0][l] + square[i][1] * cur[1][l] + square[i][2] * cur[2][l]
                nxt[i][l] = 1.5 * cur[i][l] - 0.5 * cubed
        cur = nxt
    return cur


def kernel(
    x_hbm, rot_hbm, w_hbm, dev_rows, dev_cols, tr_ref,
    rot, wv, cpart, cbuf, csend, cring, csum, hsend, hbuf, asend, abuf, bsend, bbuf, turn, rbuf, ybuf, pbuf, acc, coef, wide, dev_q,
    in_sem, c_send, c_recv, d_send, d_recv, h_send, h_recv, a_send, a_recv, b_send, b_recv, r_send, r_recv, z_send, z_recv,
    pair_send,
    y_send, y_recv, x_send, x_recv, s_send, s_recv,
):
    row = lax.axis_index("row")
    col = lax.axis_index("col")
    core = row % 2
    sibling = row + 1 - 2 * core
    y, zl = row // 8, lax.rem(row // 2, 4)
    x, zh = col // 2, lax.rem(col, 2)
    half = zl // 2
    in_half = half == zh

    def dev(x, y, zh, zl):
        return (lax.rem(y, 4) * 4 + lax.rem(zl, 4)) * 2 + core, lax.rem(x, 4) * 2 + zh

    x_ref = rbuf.at[col]
    x_load = pltpu.make_async_copy(x_hbm, x_ref, in_sem.at[0])
    rot_load = pltpu.make_async_copy(rot_hbm, rot, in_sem.at[1])
    w_load = pltpu.make_async_copy(w_hbm, wv, in_sem.at[2])
    x_load.start()
    rot_load.start()
    w_load.start()

    z = 4 * zh + zl

    def plane_peer(m):
        return dev(x + m // 4, y + m % 4, zh, zl)

    def ring_peer(m):
        there = lax.rem(z + m, 8)
        return dev(x, y, there // 4, there)

    barrier = pltpu.get_barrier_semaphore()

    def greet(r, c):
        pl.semaphore_signal(barrier, inc=1, device_id=(r, c), device_id_type=MESH)

    for m in range(1, 16):
        greet(*plane_peer(m))
    for m in range(1, 8):
        greet(*ring_peer(m))
    greet(sibling, col)

    x_load.wait()
    rot_load.wait()
    part = jnp.zeros((3, ATOMS_LOCAL), F32)
    for l in range(3):
        whole = rot[:, l, :]
        mine = jnp.zeros((3, FB), F32)
        for i in range(COLS):
            mine = mine + jnp.where(col == i, whole[:, i * FB : (i + 1) * FB], 0.0)
        block = x_ref[l * FB : (l + 1) * FB, :]
        for piece in split3(mine):
            part = part + contract(piece, block, ((1,), (0,)))
    for l in range(3):
        cpart[0:1, l * ATOMS_LOCAL : (l + 1) * ATOMS_LOCAL] = part[l : l + 1, :]

    @pl.when(x == y)
    def _():
        cbuf[x] = cpart[...]

    @pl.when(in_half)
    def _():
        ybuf[y, 2 * (zl % 2) + zh] = x_ref[...]

    pl.semaphore_wait(barrier, 23)

    def any_of(*places):
        found = z == places[0]
        for value in places[1:]:
            found = jnp.logical_or(found, z == value)
        return found

    steps = ((1, any_of(0, 1, 3, 6)), (-1, any_of(1, 4, 6, 7)), (2, any_of(1, 3)), (-2, any_of(4, 6)))

    def z_copy(m, other):
        there = lax.rem(z + 8 + steps[m][0], 8)
        h = 1 - zh if other else zh
        return remote(
            rbuf.at[2 * x + h], ybuf.at[y, 2 * lax.rem(zl, 2) + h], z_send.at[m, int(other)],
            z_recv.at[lax.rem(zl, 2), h], *dev(x, y, there // 4, there),
        )

    def for_z(other, action):
        for m in range(4):

            @pl.when(steps[m][1])
            def _():
                action(z_copy(m, other))

    def pair_copy():
        return remote(x_ref, rbuf.at[col], pair_send, r_recv.at[col], *dev(x, y, 1 - zh, zl))

    def row_copy(i, other):
        slot = 2 * x + (1 - zh if other else zh)
        source = rbuf.at[slot] if other else x_ref
        return remote(source, rbuf.at[slot], r_send.at[int(other), i], r_recv.at[slot], *dev(x + i, y, zh, zl))

    def y_copy(i, k):
        return remote(ybuf.at[y, k], ybuf.at[y, k], y_send.at[i, k], y_recv.at[y, k], *dev(x, y + i, zh, zl))

    def x_copy(i, k):
        there = lax.rem(x + i, 4)
        return remote(ybuf.at[there, k], pbuf.at[core, k, x], x_send.at[i, k], x_recv.at[k, x], *dev(there, y, zh, zl))

    def share_copy(k):
        return remote(pbuf.at[core, k], pbuf.at[core, k], s_send.at[k], s_recv.at[k], sibling, col)

    def chunk(n):
        odd = lax.rem(zl, 2)
        j = odd if n % 2 == 0 else 1 - odd
        h = zh if n < 2 else 1 - zh
        return jnp.where(in_half, 2 * j + h, (2, 1, 3, 0)[n])

    def y_forward(k):
        for i in range(1, 4):
            y_copy(i, k).start()

    def y_arrived(n):
        k = chunk(n)
        remote(x_ref, ybuf.at[y, k], pair_send, z_recv.at[k // 2, lax.rem(k, 2)], row, col).wait_recv()
        y_forward(k)

    def y_step(n):
        if n % 2:
            y_arrived(n)
        else:
            pl.when(jnp.logical_not(in_half))(lambda: y_arrived(n))

    def y_held():
        pl.when(in_half)(lambda: y_forward(chunk(2)))

    def x_step(n):
        k = chunk(n)
        for i in range(1, 4):
            there = lax.rem(x + i, 4)

            @pl.when(there != y)
            def _():
                remote(x_ref, ybuf.at[there, k], y_send.at[0, 0], y_recv.at[there, k], row, col).wait_recv()

            x_copy(i, k).start()

        @pl.when(x != y)
        def _():
            remote(x_ref, ybuf.at[x, k], y_send.at[0, 0], y_recv.at[x, k], row, col).wait_recv()

        pbuf[core, k, x] = ybuf[x, k]

    def share_step(n):
        k = chunk(n)
        for i in range(1, 4):
            there = lax.rem(x + i, 4)
            remote(x_ref, pbuf.at[core, k, there], x_send.at[0, 0], x_recv.at[k, there], row, col).wait_recv()
        share_copy(k).start()

    def centre_copy(i):
        return remote(cpart, cbuf.at[x], c_send.at[i], c_recv.at[x], *dev(y, y + i, zh, zl))

    def ring_part_copy(i):
        slot = 2 * lax.rem(zl, 2) + zh
        return remote(csend, cring.at[slot], d_send.at[i], d_recv.at[slot], *dev(x, y, half, zl + i))

    for i in range(4):
        if i:
            centre_copy(i).start()
        else:

            @pl.when(x != y)
            def _():
                centre_copy(0).start()

    pair_copy().start()
    for_z(False, lambda copy: copy.start())
    for i in range(1, 4):
        row_copy(i, False).start()

    @pl.when(in_half)
    def _():
        for i in range(1, 4):
            y_copy(i, 2 * (zl % 2) + zh).start()

    for p in range(4):

        @pl.when(jnp.logical_or(p != x, x != y))
        def _():
            remote(cpart, cbuf.at[p], c_send.at[0], c_recv.at[p], row, col).wait_recv()

    csend[...] = (cbuf[0] + cbuf[1]) + (cbuf[2] + cbuf[3])
    for i in range(4):
        if i:
            ring_part_copy(i).start()
        else:

            @pl.when(jnp.logical_not(in_half))
            def _():
                ring_part_copy(0).start()

    @pl.when(in_half)
    def _():
        cring[2 * lax.rem(zl, 2) + zh] = csend[...]

    other_slot = 2 * x + 1 - zh
    remote(x_ref, rbuf.at[other_slot], pair_send, r_recv.at[other_slot], row, col).wait_recv()
    for_z(True, lambda copy: copy.start())
    for i in range(1, 4):
        row_copy(i, True).start()

    @pl.when(in_half)
    def _():
        ybuf[y, 2 * (zl % 2) + 1 - zh] = rbuf[other_slot]


    y_step(0)
    y_step(1)
    y_held()
    for j in range(2):
        for h in range(2):

            @pl.when(jnp.logical_or(jnp.logical_not(in_half), jnp.logical_or(lax.rem(zl, 2) != j, zh != h)))
            def _():
                remote(csend, cring.at[2 * j + h], d_send.at[0], d_recv.at[2 * j + h], row, col).wait_recv()

        csum[core, j] = (cring[2 * j] + cring[2 * j + 1]) * (1.0 / FRAMES)

    def half_copy(i, src, dst):
        return remote(src, dst, h_send.at[i], h_recv.at[i], sibling, col)

    centre_half = half_copy(0, csum.at[core], csum.at[core])
    centre_half.start()
    half_copy(0, csum.at[core], csum.at[1 - core]).wait_recv()

    w_load.wait()
    lanes = [[csum[q % 2, q // 2, :, l * ATOMS_LOCAL : (l + 1) * ATOMS_LOCAL] for q in range(SUB)] for l in range(3)]

    def weigh(i, carry):
        start = pl.multiple_of(i * 32, 32)
        sums = [jnp.zeros((32, 128), F32) for _ in range(3)]
        for q in range(SUB):
            for t in range(3):
                tile = wv[pl.ds(start, 32), q * 384 + t * 128 : q * 384 + (t + 1) * 128]
                for l in range(3):
                    sums[l] = sums[l] + tile * lanes[l][q][:, t * 128 : (t + 1) * 128]
        for l in range(3):
            for p, piece in enumerate(split3(sums[l])):
                acc[pl.ds(start, 32), (3 * l + p) * 128 : (3 * l + p + 1) * 128] = piece
        return carry

    lax.fori_loop(0, 12, weigh, 0)
    shape = (8, 9 * 128)
    owner_of = lax.broadcasted_iota(jnp.int32, shape, 1) // 384
    chooser = jnp.where(owner_of == lax.broadcasted_iota(jnp.int32, shape, 0), 1.0, 0.0).astype(BF16)
    weighted = contract(chooser, acc[...], ((1,), (1,)))

    for i in range(1, 4):
        for h in range(2):
            slot = 2 * lax.rem(x + i, 4) + h
            remote(x_ref, rbuf.at[slot], r_send.at[0, 0], r_recv.at[slot], row, col).wait_recv()
    pieces = jnp.concatenate(split3(weighted), axis=0)
    first = core == 0
    for k in range(3):
        frames_k = rbuf[:, k * FB : (k + 1) * FB, :].reshape(FRAMES, ATOMS_LOCAL)
        product = contract(pieces, frames_k, ((1,), (1,)))
        product = product[0:8] + product[8:16] + product[16:24]
        own = jnp.where(first, product[:, 0:128], product[:, 128:256])
        others = jnp.where(first, product[:, 128:256], product[:, 0:128])
        for l in range(3):
            at = (3 * k + l) * 128
            asend[0:1, at : at + 128] = own[l : l + 1, :]
            hsend[0:1, at : at + 128] = others[l : l + 1, :]
    fit_half = half_copy(1, hsend, hbuf.at[0])
    fit_half.start()
    fit_half.wait_recv()
    asend[...] = asend[...] + hbuf[0]
    a_slot = 4 * x + y
    abuf[a_slot] = asend[...]

    def plane_copy(m):
        return remote(asend, abuf.at[a_slot], a_send.at[m], a_recv.at[a_slot], *plane_peer(m))

    def ring_copy(m):
        return remote(bsend, bbuf.at[z], b_send.at[m], b_recv.at[z], *ring_peer(m))

    for m in range(1, 16):
        plane_copy(m).start()
    y_step(2)
    y_step(3)
    x_step(0)
    x_step(1)
    x_step(2)
    for m in range(1, 16):
        slot = 4 * lax.rem(x + m // 4, 4) + lax.rem(y + m % 4, 4)
        remote(asend, abuf.at[slot], a_send.at[0], a_recv.at[slot], row, col).wait_recv()
    bsend[...] = jnp.sum(abuf[...], axis=0)
    bbuf[z] = bsend[...]
    for m in range(1, 8):
        ring_copy(m).start()

    share_step(0)
    share_step(1)
    x_step(3)
    centre_rows = jnp.zeros((8, ATOMS_LOCAL), F32)
    for l in range(3):
        frames_l = rbuf[:, l * FB : (l + 1) * FB, :].reshape(FRAMES, ATOMS_LOCAL)
        spin = jnp.concatenate([rot[:, l, :], jnp.zeros((5, FRAMES), F32)], axis=0)
        product = contract(jnp.concatenate(split3(spin), axis=0), frames_l, ((1,), (0,)))
        centre_rows = centre_rows + (product[0:8] + product[8:16] + product[16:24])
    centre_rows = centre_rows * (1.0 / FRAMES)

    for i in range(4):
        if i:
            centre_copy(i).wait_send()
            ring_part_copy(i).wait_send()
        else:

            @pl.when(x != y)
            def _():
                centre_copy(0).wait_send()

            @pl.when(jnp.logical_not(in_half))
            def _():
                ring_part_copy(0).wait_send()

    for m in range(1, 16):
        plane_copy(m).wait_send()
    centre_half.wait_send()
    fit_half.wait_send()
    pair_copy().wait_send()
    for_z(False, lambda copy: copy.wait_send())
    for_z(True, lambda copy: copy.wait_send())
    for i in range(1, 4):
        row_copy(i, False).wait_send()
        row_copy(i, True).wait_send()
        for n in range(3):
            y_copy(i, chunk(n)).wait_send()

    for m in range(1, 8):
        slot = lax.rem(z + m, 8)
        remote(bsend, bbuf.at[slot], b_send.at[0], b_recv.at[slot], row, col).wait_recv()
    fitted = jnp.sum(bbuf[...], axis=0)

    turned = polar_all([[fitted[:, (3 * k + l) * 128 : (3 * k + l + 1) * 128] for l in range(3)] for k in range(3)])
    for k in range(3):
        for l in range(3):
            turn[core, :, (3 * k + l) * 128 : (3 * k + l + 1) * 128] = turned[k][l]
    turn_half = half_copy(2, turn.at[core], turn.at[core])
    turn_half.start()
    share_step(2)
    half_copy(2, turn.at[core], turn.at[1 - core]).wait_recv()
    picked = jnp.where(col < 4, turn[0], turn[1])
    quarter = lax.rem(col, 4)
    for k in range(3):
        for l in range(3):
            line = picked[:, (3 * k + l) * 128 : (3 * k + l + 1) * 128]
            mine = jnp.zeros((1, FB), F32)
            for i in range(4):
                mine = mine + jnp.where(quarter == i, line[:, i * FB : (i + 1) * FB], 0.0)
            tr_ref[k, l : l + 1, :] = mine
    for half_of in range(2):
        for j in range(9):
            coef[j : j + 1, :] = turn[half_of, :, j * 128 : (j + 1) * 128]
        upright = jnp.transpose(coef[...])
        for c in range(4):
            for j in range(9):
                wide[j, 4 * half_of + c] = jnp.broadcast_to(upright[c * FB : (c + 1) * FB, j : j + 1], (FB, 128))

    def deviate(target, count, block_of, start_of, centre):
        base = [jnp.broadcast_to(centre[k], (FB, ATOMS_LOCAL)) for k in range(3)]

        def body(i, carry):
            block = block_of(i).astype(F32)
            xs = [block[l * FB : (l + 1) * FB, :] for l in range(3)]
            c = start_of(i)
            values = []
            for k in range(3):
                terms = []
                for l in range(3):
                    factor = wide[3 * k + l, c]
                    terms.append(jnp.concatenate([factor, factor, factor], axis=1) * xs[l])
                values.append((terms[0] + terms[1]) + terms[2] - base[k])
            target[pl.ds(pl.multiple_of(c * 96, 96), 96), :] = jnp.concatenate(values, axis=0).astype(BF16)
            return carry

        lax.fori_loop(0, count, body, 0)

    def deviate_piece(owner, n):
        k = chunk(n)
        j = k // 2
        centre = [csum[owner, j, :, i * ATOMS_LOCAL : (i + 1) * ATOMS_LOCAL] for i in range(3)]
        deviate(
            dev_cols.at[2 * j + owner], 4, lambda i: pbuf[owner, k, i], lambda i: 2 * i + lax.rem(k, 2), centre
        )

    def shared_wait(n):
        k = chunk(n)
        remote(pbuf.at[1 - core, k], pbuf.at[1 - core, k], s_send.at[0], s_recv.at[k], row, col).wait_recv()

    deviate(dev_q, COLS, lambda i: rbuf[i], lambda i: i, [centre_rows[k : k + 1, :] for k in range(3)])
    dev_rows[...] = jnp.transpose(dev_q[...])
    share_step(3)
    for n in range(3):
        deviate_piece(core, n)
    for n in range(3):
        shared_wait(n)
        deviate_piece(1 - core, n)
    deviate_piece(core, 3)
    shared_wait(3)
    deviate_piece(1 - core, 3)

    for m in range(1, 8):
        ring_copy(m).wait_send()
    turn_half.wait_send()
    for n in range(4):
        for i in range(1, 4):
            x_copy(i, chunk(n)).wait_send()
        share_copy(chunk(n)).wait_send()
    for i in range(1, 4):
        y_copy(i, chunk(3)).wait_send()


def multiply(rows_ref, cols_ref, tr_ref, cov_hbm, out_hbm, block, sem):
    out_copy = pltpu.make_async_copy(tr_ref, out_hbm, sem.at[SUB])
    out_copy.start()
    copies = []
    for q in range(SUB):
        block[q] = contract(rows_ref[...], cols_ref[q], ((1,), (0,))) * (1.0 / (3 * FRAMES))
        target = cov_hbm.at[:, q * ATOMS_LOCAL : (q + 1) * ATOMS_LOCAL]
        copies.append(pltpu.make_async_copy(block.at[q], target, sem.at[q]))
        copies[q].start()
    for copy in copies:
        copy.wait()
    out_copy.wait()


def per_device(frames, rotations, inverse_cov):
    x = jnp.transpose(frames, (1, 0, 2)).reshape(96, ATOMS_LOCAL)
    dma = pltpu.SemaphoreType.DMA
    vmem = pl.BlockSpec(memory_space=pltpu.VMEM)
    hbm = pl.BlockSpec(memory_space=pltpu.HBM)
    operands = [pltpu.with_memory_space_constraint(value, pltpu.HBM) for value in (x, rotations, inverse_cov)]
    dev_rows, dev_cols, turned = pl.pallas_call(
        kernel,
        out_shape=(
            jax.ShapeDtypeStruct((ATOMS_LOCAL, 3 * FRAMES), BF16),
            jax.ShapeDtypeStruct((SUB, 3 * FRAMES, ATOMS_LOCAL), BF16),
            jax.ShapeDtypeStruct((3, 3, FB), F32),
        ),
        in_specs=[hbm, hbm, hbm],
        out_specs=(vmem, vmem, vmem),
        scratch_shapes=[
            pltpu.VMEM((3, 3, 256), F32),
            pltpu.VMEM((384, 1536), F32),
            pltpu.VMEM((1, 1152), F32),
            pltpu.VMEM((4, 1, 1152), F32),
            pltpu.VMEM((1, 1152), F32),
            pltpu.VMEM((4, 1, 1152), F32),
            pltpu.VMEM((2, 2, 1, 1152), F32),
            pltpu.VMEM((1, 1152), F32),
            pltpu.VMEM((1, 1, 1152), F32),
            pltpu.VMEM((1, 1152), F32),
            pltpu.VMEM((16, 1, 1152), F32),
            pltpu.VMEM((1, 1152), F32),
            pltpu.VMEM((8, 1, 1152), F32),
            pltpu.VMEM((2, 1, 1152), F32),
            pltpu.VMEM((8, 96, 384), BF16),
            pltpu.VMEM((4, 4, 96, 384), BF16),
            pltpu.VMEM((2, 4, 4, 96, 384), BF16),
            pltpu.VMEM((384, 1152), BF16),
            pltpu.VMEM((16, 128), F32),
            pltpu.VMEM((9, 8, 32, 128), F32),
            pltpu.VMEM((768, 384), BF16),
            dma((3,)),
            dma((4,)), dma((4,)),
            dma((4,)), dma((4,)),
            dma((3,)), dma((3,)),
            dma((16,)), dma((16,)),
            dma((8,)), dma((8,)),
            dma((2, 4)), dma((8,)),
            dma((4, 2)), dma((2, 2)), dma(()),
            dma((4, 4)), dma((4, 4)),
            dma((4, 4)), dma((4, 4)),
            dma((4,)), dma((4,)),
        ],
        compiler_params=pltpu.CompilerParams(
            collective_id=0, has_side_effects=True, vmem_limit_bytes=32 * 1024 * 1024
        ),
        name="superpose",
    )(*operands)
    return pl.pallas_call(
        multiply,
        out_shape=(
            jax.ShapeDtypeStruct((ATOMS_LOCAL, SUB * ATOMS_LOCAL), F32),
            jax.ShapeDtypeStruct((3, 3, FB), F32),
        ),
        in_specs=[vmem, vmem, vmem],
        out_specs=(hbm, hbm),
        scratch_shapes=[pltpu.VMEM((SUB, ATOMS_LOCAL, ATOMS_LOCAL), F32), dma((SUB + 1,))],
        compiler_params=pltpu.CompilerParams(vmem_limit_bytes=16 * 1024 * 1024),
        name="covariance",
    )(dev_rows, dev_cols, turned)


def solution(mesh):
    placed = (P("col", None, "row"), P(), P("row", "col"))
    return jax.shard_map(
        per_device,
        mesh=mesh,
        in_specs=placed,
        out_specs=(P("row", "col"), P(None, None, "col")),
        check_vma=False,
    )
```

```python
import functools

import jax
import jax.numpy as jnp
from jax import lax
from jax.experimental import pallas as pl
from jax.experimental.pallas import tpu as pltpu
from jax.sharding import PartitionSpec as P

POLAR = 12
ROWS = 32
COLS = 8
FB = 32
SUB = 4
ATOMS_LOCAL = 384
FRAMES = ROWS * COLS
MESH = pl.DeviceIdType.MESH
F32 = jnp.float32
BF16 = jnp.bfloat16


def split3(value):
    high = value.astype(BF16)
    rest = value - high.astype(F32)
    middle = rest.astype(BF16)
    low = (rest - middle.astype(F32)).astype(BF16)
    return high, middle, low


def contract(left, right, dims):
    return lax.dot_general(left, right, (dims, ((), ())), preferred_element_type=F32)


def remote(src, dst, send, recv, row, col):
    return pltpu.make_async_remote_copy(
        src_ref=src, dst_ref=dst, send_sem=send, recv_sem=recv, device_id=(row, col), device_id_type=MESH
    )


def polar_all(fit):
    total = jnp.zeros_like(fit[0][0])
    for k in range(3):
        for l in range(3):
            total = total + fit[k][l] * fit[k][l]
    scaling = jnp.sqrt(1.0 + total)
    cur = [[fit[k][i] / scaling for k in range(3)] for i in range(3)]
    for _ in range(POLAR):
        square = [[None] * 3 for _ in range(3)]
        for i in range(3):
            for k in range(i, 3):
                value = cur[i][0] * cur[k][0] + cur[i][1] * cur[k][1] + cur[i][2] * cur[k][2]
                square[i][k] = value
                square[k][i] = value
        nxt = [[None] * 3 for _ in range(3)]
        for i in range(3):
            for l in range(3):
                cubed = square[i][0] * cur[0][l] + square[i][1] * cur[1][l] + square[i][2] * cur[2][l]
                nxt[i][l] = 1.5 * cur[i][l] - 0.5 * cubed
        cur = nxt
    return cur


def kernel(
    x_hbm, rot_hbm, w_hbm, dev_rows, dev_cols, tr_ref,
    rot, wv, cpart, cbuf, csend, cring, csum, hsend, hbuf, asend, abuf, bsend, bbuf, turn, rbuf, ybuf, pbuf, acc, coef, wide, dev_q,
    in_sem, c_send, c_recv, d_send, d_recv, h_send, h_recv, a_send, a_recv, b_send, b_recv, r_send, r_recv, z_send, z_recv,
    pair_send,
    y_send, y_recv, x_send, x_recv, s_send, s_recv,
):
    row = lax.axis_index("row")
    col = lax.axis_index("col")
    core = row % 2
    sibling = row + 1 - 2 * core
    y, zl = row // 8, lax.rem(row // 2, 4)
    x, zh = col // 2, lax.rem(col, 2)
    half = zl // 2
    in_half = half == zh

    def dev(x, y, zh, zl):
        return (lax.rem(y, 4) * 4 + lax.rem(zl, 4)) * 2 + core, lax.rem(x, 4) * 2 + zh

    x_ref = rbuf.at[col]
    x_load = pltpu.make_async_copy(x_hbm, x_ref, in_sem.at[0])
    rot_load = pltpu.make_async_copy(rot_hbm, rot, in_sem.at[1])
    w_load = pltpu.make_async_copy(w_hbm, wv, in_sem.at[2])
    x_load.start()
    rot_load.start()
    w_load.start()

    z = 4 * zh + zl

    def plane_peer(m):
        return dev(x + m // 4, y + m % 4, zh, zl)

    def ring_peer(m):
        there = lax.rem(z + m, 8)
        return dev(x, y, there // 4, there)

    barrier = pltpu.get_barrier_semaphore()

    def greet(r, c):
        pl.semaphore_signal(barrier, inc=1, device_id=(r, c), device_id_type=MESH)

    for m in range(1, 16):
        greet(*plane_peer(m))
    for m in range(1, 8):
        greet(*ring_peer(m))
    greet(sibling, col)

    x_load.wait()
    rot_load.wait()
    part = jnp.zeros((3, ATOMS_LOCAL), F32)
    for l in range(3):
        whole = rot[:, l, :]
        mine = jnp.zeros((3, FB), F32)
        for i in range(COLS):
            mine = mine + jnp.where(col == i, whole[:, i * FB : (i + 1) * FB], 0.0)
        block = x_ref[l * FB : (l + 1) * FB, :]
        for piece in split3(mine):
            part = part + contract(piece, block, ((1,), (0,)))
    for l in range(3):
        cpart[0:1, l * ATOMS_LOCAL : (l + 1) * ATOMS_LOCAL] = part[l : l + 1, :]

    @pl.when(x == y)
    def _():
        cbuf[x] = cpart[...]

    @pl.when(in_half)
    def _():
        ybuf[y, 2 * (zl % 2) + zh] = x_ref[...]

    pl.semaphore_wait(barrier, 23)

    def any_of(*places):
        found = z == places[0]
        for value in places[1:]:
            found = jnp.logical_or(found, z == value)
        return found

    steps = ((1, any_of(0, 1, 3, 6)), (-1, any_of(1, 4, 6, 7)), (2, any_of(1, 3)), (-2, any_of(4, 6)))

    def z_copy(m, other):
        there = lax.rem(z + 8 + steps[m][0], 8)
        h = 1 - zh if other else zh
        return remote(
            rbuf.at[2 * x + h], ybuf.at[y, 2 * lax.rem(zl, 2) + h], z_send.at[m, int(other)],
            z_recv.at[lax.rem(zl, 2), h], *dev(x, y, there // 4, there),
        )

    def for_z(other, action):
        for m in range(4):

            @pl.when(steps[m][1])
            def _():
                action(z_copy(m, other))

    def pair_copy():
        return remote(x_ref, rbuf.at[col], pair_send, r_recv.at[col], *dev(x, y, 1 - zh, zl))

    def row_copy(i, other):
        slot = 2 * x + (1 - zh if other else zh)
        source = rbuf.at[slot] if other else x_ref
        return remote(source, rbuf.at[slot], r_send.at[int(other), i], r_recv.at[slot], *dev(x + i, y, zh, zl))

    def y_copy(i, k):
        return remote(ybuf.at[y, k], ybuf.at[y, k], y_send.at[i, k], y_recv.at[y, k], *dev(x, y + i, zh, zl))

    def x_copy(i, k):
        there = lax.rem(x + i, 4)
        return remote(ybuf.at[there, k], pbuf.at[core, k, x], x_send.at[i, k], x_recv.at[k, x], *dev(there, y, zh, zl))

    def share_copy(k):
        return remote(pbuf.at[core, k], pbuf.at[core, k], s_send.at[k], s_recv.at[k], sibling, col)

    def chunk(n):
        odd = lax.rem(zl, 2)
        j = odd if n % 2 == 0 else 1 - odd
        h = zh if n < 2 else 1 - zh
        return jnp.where(in_half, 2 * j + h, (2, 1, 3, 0)[n])

    def y_forward(k):
        for i in range(1, 4):
            y_copy(i, k).start()

    def y_arrived(n):
        k = chunk(n)
        remote(x_ref, ybuf.at[y, k], pair_send, z_recv.at[k // 2, lax.rem(k, 2)], row, col).wait_recv()
        y_forward(k)

    def y_step(n):
        if n % 2:
            y_arrived(n)
        else:
            pl.when(jnp.logical_not(in_half))(lambda: y_arrived(n))

    def y_held():
        pl.when(in_half)(lambda: y_forward(chunk(2)))

    def x_step(n):
        k = chunk(n)
        for i in range(1, 4):
            there = lax.rem(x + i, 4)

            @pl.when(there != y)
            def _():
                remote(x_ref, ybuf.at[there, k], y_send.at[0, 0], y_recv.at[there, k], row, col).wait_recv()

            x_copy(i, k).start()

        @pl.when(x != y)
        def _():
            remote(x_ref, ybuf.at[x, k], y_send.at[0, 0], y_recv.at[x, k], row, col).wait_recv()

        pbuf[core, k, x] = ybuf[x, k]

    def share_step(n):
        k = chunk(n)
        for i in range(1, 4):
            there = lax.rem(x + i, 4)
            remote(x_ref, pbuf.at[core, k, there], x_send.at[0, 0], x_recv.at[k, there], row, col).wait_recv()
        share_copy(k).start()

    def centre_copy(i):
        return remote(cpart, cbuf.at[x], c_send.at[i], c_recv.at[x], *dev(y, y + i, zh, zl))

    def ring_part_copy(i):
        slot = 2 * lax.rem(zl, 2) + zh
        return remote(csend, cring.at[slot], d_send.at[i], d_recv.at[slot], *dev(x, y, half, zl + i))

    for i in range(4):
        if i:
            centre_copy(i).start()
        else:

            @pl.when(x != y)
            def _():
                centre_copy(0).start()

    pair_copy().start()
    for_z(False, lambda copy: copy.start())
    for i in range(1, 4):
        row_copy(i, False).start()

    @pl.when(in_half)
    def _():
        for i in range(1, 4):
            y_copy(i, 2 * (zl % 2) + zh).start()

    for p in range(4):

        @pl.when(jnp.logical_or(p != x, x != y))
        def _():
            remote(cpart, cbuf.at[p], c_send.at[0], c_recv.at[p], row, col).wait_recv()

    csend[...] = (cbuf[0] + cbuf[1]) + (cbuf[2] + cbuf[3])
    for i in range(4):
        if i:
            ring_part_copy(i).start()
        else:

            @pl.when(jnp.logical_not(in_half))
            def _():
                ring_part_copy(0).start()

    @pl.when(in_half)
    def _():
        cring[2 * lax.rem(zl, 2) + zh] = csend[...]

    other_slot = 2 * x + 1 - zh
    remote(x_ref, rbuf.at[other_slot], pair_send, r_recv.at[other_slot], row, col).wait_recv()
    for_z(True, lambda copy: copy.start())
    for i in range(1, 4):
        row_copy(i, True).start()

    @pl.when(in_half)
    def _():
        ybuf[y, 2 * (zl % 2) + 1 - zh] = rbuf[other_slot]


    y_step(0)
    y_step(1)
    y_held()
    for j in range(2):
        for h in range(2):

            @pl.when(jnp.logical_or(jnp.logical_not(in_half), jnp.logical_or(lax.rem(zl, 2) != j, zh != h)))
            def _():
                remote(csend, cring.at[2 * j + h], d_send.at[0], d_recv.at[2 * j + h], row, col).wait_recv()

        csum[core, j] = (cring[2 * j] + cring[2 * j + 1]) * (1.0 / FRAMES)

    def half_copy(i, src, dst):
        return remote(src, dst, h_send.at[i], h_recv.at[i], sibling, col)

    centre_half = half_copy(0, csum.at[core], csum.at[core])
    centre_half.start()
    half_copy(0, csum.at[core], csum.at[1 - core]).wait_recv()

    w_load.wait()
    lanes = [[csum[q % 2, q // 2, :, l * ATOMS_LOCAL : (l + 1) * ATOMS_LOCAL] for q in range(SUB)] for l in range(3)]

    def weigh(i, carry):
        start = pl.multiple_of(i * 32, 32)
        sums = [jnp.zeros((32, 128), F32) for _ in range(3)]
        for q in range(SUB):
            for t in range(3):
                tile = wv[pl.ds(start, 32), q * 384 + t * 128 : q * 384 + (t + 1) * 128]
                for l in range(3):
                    sums[l] = sums[l] + tile * lanes[l][q][:, t * 128 : (t + 1) * 128]
        for l in range(3):
            for p, piece in enumerate(split3(sums[l])):
                acc[pl.ds(start, 32), (3 * l + p) * 128 : (3 * l + p + 1) * 128] = piece
        return carry

    lax.fori_loop(0, 12, weigh, 0)
    shape = (8, 9 * 128)
    owner_of = lax.broadcasted_iota(jnp.int32, shape, 1) // 384
    chooser = jnp.where(owner_of == lax.broadcasted_iota(jnp.int32, shape, 0), 1.0, 0.0).astype(BF16)
    weighted = contract(chooser, acc[...], ((1,), (1,)))

    for i in range(1, 4):
        for h in range(2):
            slot = 2 * lax.rem(x + i, 4) + h
            remote(x_ref, rbuf.at[slot], r_send.at[0, 0], r_recv.at[slot], row, col).wait_recv()
    pieces = jnp.concatenate(split3(weighted), axis=0)
    first = core == 0
    for k in range(3):
        frames_k = rbuf[:, k * FB : (k + 1) * FB, :].reshape(FRAMES, ATOMS_LOCAL)
        product = contract(pieces, frames_k, ((1,), (1,)))
        product = product[0:8] + product[8:16] + product[16:24]
        own = jnp.where(first, product[:, 0:128], product[:, 128:256])
        others = jnp.where(first, product[:, 128:256], product[:, 0:128])
        for l in range(3):
            at = (3 * k + l) * 128
            asend[0:1, at : at + 128] = own[l : l + 1, :]
            hsend[0:1, at : at + 128] = others[l : l + 1, :]
    fit_half = half_copy(1, hsend, hbuf.at[0])
    fit_half.start()
    fit_half.wait_recv()
    asend[...] = asend[...] + hbuf[0]
    a_slot = 4 * x + y
    abuf[a_slot] = asend[...]

    def plane_copy(m):
        return remote(asend, abuf.at[a_slot], a_send.at[m], a_recv.at[a_slot], *plane_peer(m))

    def ring_copy(m):
        return remote(bsend, bbuf.at[z], b_send.at[m], b_recv.at[z], *ring_peer(m))

    for m in range(1, 16):
        plane_copy(m).start()
    y_step(2)
    y_step(3)
    x_step(0)
    x_step(1)
    x_step(2)
    for m in range(1, 16):
        slot = 4 * lax.rem(x + m // 4, 4) + lax.rem(y + m % 4, 4)
        remote(asend, abuf.at[slot], a_send.at[0], a_recv.at[slot], row, col).wait_recv()
    bsend[...] = jnp.sum(abuf[...], axis=0)
    bbuf[z] = bsend[...]
    for m in range(1, 8):
        ring_copy(m).start()

    share_step(0)
    share_step(1)
    x_step(3)
    centre_rows = jnp.zeros((8, ATOMS_LOCAL), F32)
    for l in range(3):
        frames_l = rbuf[:, l * FB : (l + 1) * FB, :].reshape(FRAMES, ATOMS_LOCAL)
        spin = jnp.concatenate([rot[:, l, :], jnp.zeros((5, FRAMES), F32)], axis=0)
        product = contract(jnp.concatenate(split3(spin), axis=0), frames_l, ((1,), (0,)))
        centre_rows = centre_rows + (product[0:8] + product[8:16] + product[16:24])
    centre_rows = centre_rows * (1.0 / FRAMES)

    for i in range(4):
        if i:
            centre_copy(i).wait_send()
            ring_part_copy(i).wait_send()
        else:

            @pl.when(x != y)
            def _():
                centre_copy(0).wait_send()

            @pl.when(jnp.logical_not(in_half))
            def _():
                ring_part_copy(0).wait_send()

    for m in range(1, 16):
        plane_copy(m).wait_send()
    centre_half.wait_send()
    fit_half.wait_send()
    pair_copy().wait_send()
    for_z(False, lambda copy: copy.wait_send())
    for_z(True, lambda copy: copy.wait_send())
    for i in range(1, 4):
        row_copy(i, False).wait_send()
        row_copy(i, True).wait_send()
        for n in range(3):
            y_copy(i, chunk(n)).wait_send()

    for m in range(1, 8):
        slot = lax.rem(z + m, 8)
        remote(bsend, bbuf.at[slot], b_send.at[0], b_recv.at[slot], row, col).wait_recv()
    fitted = jnp.sum(bbuf[...], axis=0)

    turned = polar_all([[fitted[:, (3 * k + l) * 128 : (3 * k + l + 1) * 128] for l in range(3)] for k in range(3)])
    for k in range(3):
        for l in range(3):
            turn[core, :, (3 * k + l) * 128 : (3 * k + l + 1) * 128] = turned[k][l]
    turn_half = half_copy(2, turn.at[core], turn.at[core])
    turn_half.start()
    share_step(2)
    half_copy(2, turn.at[core], turn.at[1 - core]).wait_recv()
    picked = jnp.where(col < 4, turn[0], turn[1])
    quarter = lax.rem(col, 4)
    for k in range(3):
        for l in range(3):
            line = picked[:, (3 * k + l) * 128 : (3 * k + l + 1) * 128]
            mine = jnp.zeros((1, FB), F32)
            for i in range(4):
                mine = mine + jnp.where(quarter == i, line[:, i * FB : (i + 1) * FB], 0.0)
            tr_ref[k, l : l + 1, :] = mine
    for half_of in range(2):
        for j in range(9):
            coef[j : j + 1, :] = turn[half_of, :, j * 128 : (j + 1) * 128]
        upright = jnp.transpose(coef[...])
        for c in range(4):
            for j in range(9):
                wide[j, 4 * half_of + c] = jnp.broadcast_to(upright[c * FB : (c + 1) * FB, j : j + 1], (FB, 128))

    def deviate(target, count, block_of, start_of, centre):
        base = [jnp.broadcast_to(centre[k], (FB, ATOMS_LOCAL)) for k in range(3)]

        def body(i, carry):
            block = block_of(i).astype(F32)
            xs = [block[l * FB : (l + 1) * FB, :] for l in range(3)]
            c = start_of(i)
            values = []
            for k in range(3):
                terms = []
                for l in range(3):
                    factor = wide[3 * k + l, c]
                    terms.append(jnp.concatenate([factor, factor, factor], axis=1) * xs[l])
                values.append((terms[0] + terms[1]) + terms[2] - base[k])
            target[pl.ds(pl.multiple_of(c * 96, 96), 96), :] = jnp.concatenate(values, axis=0).astype(BF16)
            return carry

        lax.fori_loop(0, count, body, 0)

    def deviate_piece(owner, n):
        k = chunk(n)
        j = k // 2
        centre = [csum[owner, j, :, i * ATOMS_LOCAL : (i + 1) * ATOMS_LOCAL] for i in range(3)]
        deviate(
            dev_cols.at[2 * j + owner], 4, lambda i: pbuf[owner, k, i], lambda i: 2 * i + lax.rem(k, 2), centre
        )

    def shared_wait(n):
        k = chunk(n)
        remote(pbuf.at[1 - core, k], pbuf.at[1 - core, k], s_send.at[0], s_recv.at[k], row, col).wait_recv()

    share_step(3)
    deviate(dev_q, COLS, lambda i: rbuf[i], lambda i: i, [centre_rows[k : k + 1, :] for k in range(3)])
    for n in range(3):
        deviate_piece(core, n)
    for n in range(3):
        shared_wait(n)
        deviate_piece(1 - core, n)
    dev_rows[...] = jnp.transpose(dev_q[...])
    deviate_piece(core, 3)
    shared_wait(3)
    deviate_piece(1 - core, 3)

    for m in range(1, 8):
        ring_copy(m).wait_send()
    turn_half.wait_send()
    for n in range(4):
        for i in range(1, 4):
            x_copy(i, chunk(n)).wait_send()
        share_copy(chunk(n)).wait_send()
    for i in range(1, 4):
        y_copy(i, chunk(3)).wait_send()


def multiply(rows_ref, cols_ref, tr_ref, cov_hbm, out_hbm, block, sem):
    out_copy = pltpu.make_async_copy(tr_ref, out_hbm, sem.at[SUB])
    out_copy.start()
    copies = []
    for q in range(SUB):
        block[q] = contract(rows_ref[...], cols_ref[q], ((1,), (0,))) * (1.0 / (3 * FRAMES))
        target = cov_hbm.at[:, q * ATOMS_LOCAL : (q + 1) * ATOMS_LOCAL]
        copies.append(pltpu.make_async_copy(block.at[q], target, sem.at[q]))
        copies[q].start()
    for copy in copies:
        copy.wait()
    out_copy.wait()


def per_device(frames, rotations, inverse_cov):
    x = jnp.transpose(frames, (1, 0, 2)).reshape(96, ATOMS_LOCAL)
    dma = pltpu.SemaphoreType.DMA
    vmem = pl.BlockSpec(memory_space=pltpu.VMEM)
    hbm = pl.BlockSpec(memory_space=pltpu.HBM)
    operands = [pltpu.with_memory_space_constraint(value, pltpu.HBM) for value in (x, rotations, inverse_cov)]
    dev_rows, dev_cols, turned = pl.pallas_call(
        kernel,
        out_shape=(
            jax.ShapeDtypeStruct((ATOMS_LOCAL, 3 * FRAMES), BF16),
            jax.ShapeDtypeStruct((SUB, 3 * FRAMES, ATOMS_LOCAL), BF16),
            jax.ShapeDtypeStruct((3, 3, FB), F32),
        ),
        in_specs=[hbm, hbm, hbm],
        out_specs=(vmem, vmem, vmem),
        scratch_shapes=[
            pltpu.VMEM((3, 3, 256), F32),
            pltpu.VMEM((384, 1536), F32),
            pltpu.VMEM((1, 1152), F32),
            pltpu.VMEM((4, 1, 1152), F32),
            pltpu.VMEM((1, 1152), F32),
            pltpu.VMEM((4, 1, 1152), F32),
            pltpu.VMEM((2, 2, 1, 1152), F32),
            pltpu.VMEM((1, 1152), F32),
            pltpu.VMEM((1, 1, 1152), F32),
            pltpu.VMEM((1, 1152), F32),
            pltpu.VMEM((16, 1, 1152), F32),
            pltpu.VMEM((1, 1152), F32),
            pltpu.VMEM((8, 1, 1152), F32),
            pltpu.VMEM((2, 1, 1152), F32),
            pltpu.VMEM((8, 96, 384), BF16),
            pltpu.VMEM((4, 4, 96, 384), BF16),
            pltpu.VMEM((2, 4, 4, 96, 384), BF16),
            pltpu.VMEM((384, 1152), BF16),
            pltpu.VMEM((16, 128), F32),
            pltpu.VMEM((9, 8, 32, 128), F32),
            pltpu.VMEM((768, 384), BF16),
            dma((3,)),
            dma((4,)), dma((4,)),
            dma((4,)), dma((4,)),
            dma((3,)), dma((3,)),
            dma((16,)), dma((16,)),
            dma((8,)), dma((8,)),
            dma((2, 4)), dma((8,)),
            dma((4, 2)), dma((2, 2)), dma(()),
            dma((4, 4)), dma((4, 4)),
            dma((4, 4)), dma((4, 4)),
            dma((4,)), dma((4,)),
        ],
        compiler_params=pltpu.CompilerParams(
            collective_id=0, has_side_effects=True, vmem_limit_bytes=32 * 1024 * 1024
        ),
        name="superpose",
    )(*operands)
    return pl.pallas_call(
        multiply,
        out_shape=(
            jax.ShapeDtypeStruct((ATOMS_LOCAL, SUB * ATOMS_LOCAL), F32),
            jax.ShapeDtypeStruct((3, 3, FB), F32),
        ),
        in_specs=[vmem, vmem, vmem],
        out_specs=(hbm, hbm),
        scratch_shapes=[pltpu.VMEM((SUB, ATOMS_LOCAL, ATOMS_LOCAL), F32), dma((SUB + 1,))],
        compiler_params=pltpu.CompilerParams(vmem_limit_bytes=16 * 1024 * 1024),
        name="covariance",
    )(dev_rows, dev_cols, turned)


def solution(mesh):
    placed = (P("col", None, "row"), P(), P("row", "col"))
    return jax.shard_map(
        per_device,
        mesh=mesh,
        in_specs=placed,
        out_specs=(P("row", "col"), P(None, None, "col")),
        check_vma=False,
    )
```
